32 devices in a mesh: rows: 32 (over z, y, x, core).
Axes of the slice: x: 2, y: 2, z: 4, core: 2. Of those that a mesh axis runs over, the one named last changes fastest.
Arguments:
- diag_noise: bfloat16 [448, 128, 128], P('rows'), may hold values from -1 to 1
- couplings: bfloat16 [448, 3, 128, 128], P('rows'), may hold values from -1 to 1
- shifts: bfloat16 [448, 128], P('rows'), may hold values from 1.5 to 3
- near_devices: int32 [448, 3], P('rows'), may hold values from 0 to 30, all different within a row; in each aligned block of 14 rows (0 to 13, 14 to 27, ...) at most 3 rows name the same one
- near_slots: int32 [448, 3], P('rows'), may hold values from 0 to 13
- vectors: float32 [32, 57344], P(None, 'rows'), may hold values from -6 to 6
Outputs:
- transformed: float32 [32, 57344], P(None, 'rows')
The draws below stay inside these ranges and needn't reach their ends.
Inputs may be any that keep to these rules, and one draw needn't show every extreme that they name: `near_devices`: each row names three different distances. Among the 14 block rows of one device, no distance is named by more than 3 rows, and in some such group one distance is named by exactly 3 rows.
All inputs are finite; a program needn't handle non-finite values.
Results may differ from the reference program's by a relative error of at most 0.0014.
Values may be sent and summed in bfloat16 or wider, within the bound.
A program may use at most 128 MiB of HBM per device.

```python
import math
import jax
import jax.numpy as jnp
import numpy as np
from jax import lax

BLK = 128
NVEC = 32
RB = 14
NB = 448
PEERS = 31
CAP = 3
N_ROWS = 32


def random_signs(key, shape):
    return jnp.where(jax.random.bernoulli(key, 0.5, shape), 1.0, -1.0).astype(jnp.float32)


def draw_diag_noise(key, part):
    values = jax.random.uniform(jax.random.fold_in(key, 101), (NB, BLK, BLK), jnp.float32, -1.0, 1.0)
    signs = random_signs(jax.random.fold_in(key, 103), (NB, BLK))
    shared = signs[:, :, None] * signs[:, None, :]
    values = 0.25 * shared + 0.75 * values
    return values.astype(jnp.bfloat16)


def draw_couplings(key, part):
    values = jax.random.uniform(jax.random.fold_in(key, 201), (NB, 3, BLK, BLK), jnp.float32, -1.0, 1.0)
    row_signs = random_signs(jax.random.fold_in(key, 203), (NB, 1, BLK))
    col_signs = random_signs(jax.random.fold_in(key, 204), (NB, 3, BLK))
    shared = row_signs[:, :, :, None] * col_signs[:, :, None, :]
    values = 0.15 * shared + 0.85 * values
    return values.astype(jnp.bfloat16)


def set_ends(values, key, smallest, high):
    longest = values.shape.index(max(values.shape))
    spots = []
    for shift in (0, 1):
        where = [jax.random.randint(jax.random.fold_in(key, axis), (), 0, length) for axis, length in enumerate(values.shape)]
        where[longest] = (where[longest] + shift) % values.shape[longest]
        spots.append(tuple(where))
    return values.at[spots[0]].set(smallest).at[spots[1]].set(high)


def block_scale(key, dims, split, low, high):
    def one(dim, blocks):
        steps = jax.random.uniform(jax.random.fold_in(jax.random.fold_in(key, 6), dim), (blocks,), jnp.float32, low / len(split), high / len(split))
        return jnp.repeat(jnp.exp(steps), dims[dim] // blocks).reshape((-1,) + (1,) * (len(dims) - dim - 1))

    loudness = one(*split[0])
    for cut in split[1:]:
        loudness = loudness * one(*cut)
    return loudness


def shared_out(stream_key, own, number, rows, number_of, top, reach, slope):
    ranking = jax.random.permutation(stream_key, number_of)
    crowded, ordinary = load_shares(number_of, rows * top, reach, slope, True), load_shares(number_of, rows * top, reach, slope, False)
    places = jnp.arange(number_of)

    def named(tallies, offset_by):
        used = int((tallies > 0).sum())
        fixed = max(1, used // 4)
        passed = fixed + (places - fixed + offset_by * (used - fixed)) % max(1, number_of - fixed)
        return jnp.zeros((number_of,), jnp.int32).at[ranking[jnp.where(places < fixed, places, passed)]].set(jnp.asarray(tallies, jnp.int32))

    tallies = jnp.where(number % 4 == 0, named(crowded, number // 4), named(ordinary, number - number // 4 - 1))
    mixed = jax.random.permutation(jax.random.fold_in(own, 3), number_of)
    source_of, taker = mixed[0:number_of // 2 * 2:2], mixed[1:number_of // 2 * 2:2]
    slack = jnp.minimum(tallies[source_of] - 1, reach - tallies[taker]) // 2
    slack = jnp.where((source_of == ranking[0]) | (taker == ranking[0]) | (tallies[taker] == 0), 0, jnp.maximum(slack, 0))
    passed = jax.random.randint(jax.random.fold_in(own, 4), (number_of // 2,), 0, 1 << 20) % (slack + 1)
    tallies = tallies.at[source_of].add(-passed).at[taker].add(passed)
    members = jnp.searchsorted(jnp.cumsum(tallies), jnp.arange(rows * top), side="right").astype(jnp.int32)
    grid = members.reshape(top, rows).T
    grid = grid[jax.random.permutation(jax.random.fold_in(own, 1), rows)]
    offset_by = jax.random.randint(jax.random.fold_in(own, 2), (rows, 1), 0, top)
    return jnp.take_along_axis(grid, (jnp.arange(top)[None, :] + offset_by) % top, axis=1)


def load_shares(amount, total, limit, slope, full):
    portions = [(1 << 20) // math.isqrt(grade ** slope) + 1 for grade in range(1, amount + 1)]
    largest = limit if full else min(limit, max(-(-total // amount), total * portions[0] // sum(portions)))
    least = 1 if total - largest >= amount - 1 else 0
    given, spare = [largest] + [least] * (amount - 1), total - largest - least * (amount - 1)
    while spare > 0:
        movable = [i for i in range(1, amount) if given[i] < largest] or [i for i in range(1, amount) if given[i] < limit]
        whole, remaining = sum([portions[i] for i in movable]), spare
        for i in movable:
            addition = min(limit - given[i], max(1, remaining * portions[i] // whole), spare)
            given[i] = given[i] + addition
            spare = spare - addition
    return np.array(given)


def normal_values(key, extent, width, limit, shards=(), kind=jnp.bfloat16):
    values = jax.random.normal(key, extent, jnp.float32) * width
    if len(shards) > 0:
        values = block_scale(key, extent, shards, -0.22, 0.18) * values
    return jnp.clip(values, min=-limit, max=limit).astype(kind)


def setup_inputs(seed: int = 0) -> dict:
    splits = jax.random.split(jax.random.key(seed), 7)
    diag_noise = draw_diag_noise(jax.random.fold_in(splits[6], 71), 0)
    couplings = draw_couplings(jax.random.fold_in(splits[6], 71), 0)
    shifts = jnp.clip(jnp.exp(math.log(3.0) - 0.6931472 * jax.random.uniform(splits[2], (NB, BLK), jnp.float32) ** block_scale(splits[2], (NB, BLK), ((0, 32),), -0.2, 0.2)), 1.5, 3.0).astype(jnp.bfloat16)
    near_devices_keys = jax.random.split(jax.random.fold_in(splits[3], 1), NB // RB)
    near_devices_turns = jax.random.permutation(jax.random.fold_in(splits[3], 3), NB // RB)
    near_devices = jax.vmap(lambda own, number: shared_out(jax.random.fold_in(splits[3], 2), own, number, RB, PEERS, 3, CAP, 0))(near_devices_keys, near_devices_turns).reshape((NB, 3))
    near_slots = set_ends(jax.random.randint(splits[4], (NB, 3), 0, RB), jax.random.fold_in(splits[4], 1), 0, RB - 1).astype(jnp.int32)
    vectors = normal_values(splits[5], (NVEC, NB * BLK), 1.0, 6.0, ((1, 32),), jnp.float32)
    return dict(diag_noise=diag_noise, couplings=couplings, shifts=shifts, near_devices=near_devices, near_slots=near_slots, vectors=vectors)


highest = lax.Precision.HIGHEST

def invert(matrix):
    lower_factor = jnp.linalg.cholesky(matrix)
    identity = jnp.broadcast_to(jnp.eye(matrix.shape[-1], dtype=matrix.dtype), matrix.shape)
    inverse_lower = jax.scipy.linalg.solve_triangular(lower_factor, identity, lower=True)
    return jnp.einsum('...ba,...bc->...ac', inverse_lower, inverse_lower, precision=highest)

def build_diag(noise_block, shift_block, factor):
    noise_block = noise_block.astype(jnp.float32) * factor
    symmetric = (noise_block + jnp.swapaxes(noise_block, -1, -2)) * 0.5
    eye_block = jnp.eye(noise_block.shape[-1], dtype=jnp.float32)
    return symmetric + shift_block.astype(jnp.float32)[..., :, None] * eye_block

def row_factors(diag_own, coupling, inverse_near):
    product = jnp.einsum('rmab,rmbc->rmac', coupling, inverse_near, precision=highest)
    schur_block = diag_own - jnp.einsum('rmab,rmcb->rac', product, coupling, precision=highest)
    lower_factor = jnp.linalg.cholesky(invert(schur_block))
    factor_diag = jnp.swapaxes(lower_factor, -1, -2)
    factor_off = -jnp.einsum('rba,rmbc->rmac', lower_factor, product, precision=highest)
    return (factor_diag, factor_off)

def reference(diag_noise, couplings, shifts, near_devices, near_slots, vectors):
    factor = 0.5 / math.sqrt(BLK)
    coupling_factor = 0.4 / math.sqrt(BLK)
    owner_device = jnp.arange(NB, dtype=jnp.int32) // RB
    near_index = ((owner_device[:, None] - 1 - near_devices) % N_ROWS * RB + near_slots).astype(jnp.int32)
    inverse_all = invert(build_diag(diag_noise, shifts, factor))
    noise_spans = diag_noise.reshape(N_ROWS, RB, BLK, BLK)
    shift_spans = shifts.reshape(N_ROWS, RB, BLK)
    coupling_spans = couplings.reshape(N_ROWS, RB, 3, BLK, BLK)
    index_spans = near_index.reshape(N_ROWS, RB, 3)

    def setup_block(pieces):
        noise_block, shift_block, coupling_raw, index_block = pieces
        diag_own = build_diag(noise_block, shift_block, factor)
        coupling = coupling_raw.astype(jnp.float32) * coupling_factor
        return row_factors(diag_own, coupling, inverse_all[index_block])
    factor_diag, factor_off = lax.map(setup_block, (noise_spans, shift_spans, coupling_spans, index_spans))
    factor_diag = factor_diag.reshape(NB, BLK, BLK)
    factor_off = factor_off.reshape(NB, 3, BLK, BLK)
    vector_rows = vectors.reshape(NVEC, NB, BLK).transpose(1, 0, 2)
    left_product = jnp.einsum('rva,rab->rvb', vector_rows, factor_diag, precision=highest)
    outgoing = jnp.einsum('rva,rmab->rmvb', vector_rows, factor_off, precision=highest)
    left_product = left_product.at[near_index].add(outgoing)

    def coupling_block(pieces):
        noise_block, shift_block, coupling_raw, index_block, left_block = pieces
        diag_own = build_diag(noise_block, shift_block, factor)
        coupling = coupling_raw.astype(jnp.float32) * coupling_factor
        middle = jnp.einsum('rva,rab->rvb', left_block, diag_own, precision=highest)
        middle = middle + jnp.einsum('rmvb,rmab->rva', left_product[index_block], coupling, precision=highest)
        pushed = jnp.einsum('rva,rmab->rmvb', left_block, coupling, precision=highest)
        return (middle, pushed)
    middle_product, pushed = lax.map(coupling_block, (noise_spans, shift_spans, coupling_spans, index_spans, left_product.reshape(N_ROWS, RB, NVEC, BLK)))
    middle_product = middle_product.reshape(NB, NVEC, BLK).at[near_index].add(pushed.reshape(NB, 3, NVEC, BLK))
    result = jnp.einsum('rvb,rab->rva', middle_product, factor_diag, precision=highest)
    result = result + jnp.einsum('rmvb,rmab->rva', middle_product[near_index], factor_off, precision=highest)
    return result.transpose(1, 0, 2).reshape(NVEC, NB * BLK)
```

```python
import functools
import math

import jax
import jax.numpy as jnp
from jax import lax
from jax.experimental import pallas as pl
from jax.experimental.pallas import tpu as pltpu
from jax.sharding import PartitionSpec as P

PANEL = 16
GROUP = 4
LAYERS = 4
TAIL = 16
MESH = pl.DeviceIdType.MESH
bf16, f32 = jnp.bfloat16, jnp.float32


def split2(x):
    high = x.astype(bf16)
    return high, (x - high.astype(f32)).astype(bf16)


def joined(*parts):
    return jnp.concatenate(parts, axis=-1)


def tdot(a, b):
    return lax.dot_general(a, b, (((0,), (0,)), ((), ())), preferred_element_type=f32)


def dot_nn(a, b):
    return jnp.dot(a, b, preferred_element_type=f32)


def dot_nt(a, b):
    return lax.dot_general(a, b, (((1,), (1,)), ((), ())), preferred_element_type=f32)


def eliminate(m, pscr, qscr, count, pad, size):
    panel = PANEL
    lane = lax.broadcasted_iota(jnp.int32, (pad, size), 1)
    for block in reversed(range(size // panel)):
        base = block * panel
        rows = [m[pl.ds(base + r, pad, stride=size), :] for r in range(panel)]
        for k in reversed(range(panel)):
            col = base + k
            here = lane == col
            if (k + 1) % GROUP == 0:
                first = k + 1 - GROUP
                tile = {
                    (i, c): jnp.broadcast_to(rows[i][:, base + c : base + c + 1], (pad, size))
                    for c in range(first, k + 1)
                    for i in range(c + 1)
                }
            inv = 1.0 / tile[k, k]
            for c in reversed(range(first, k)):
                ratio = tile[c, k] * inv
                for i in range(c + 1):
                    tile[i, c] = tile[i, c] - tile[i, k] * ratio
            pivot_row = jnp.where(here, 1.0, rows[k])
            scaled = pivot_row * inv
            for i in range(k):
                rows[i] = jnp.where(here, 0.0, rows[i]) - tile[i, k] * scaled
            if block:
                pscr[pl.ds(k * pad, pad), :] = jnp.where(
                    (lane >= base) & (lane < col), 0.0, pivot_row
                )
                qscr[pl.ds(k * pad, pad), :] = scaled
            m[pl.ds(col, pad, stride=size), :] = jnp.where(
                lane >= col, pivot_row * jnp.sqrt(inv), 0.0
            )
        if block:
            lane_m = lax.broadcasted_iota(jnp.int32, (base, size), 1)
            inside = (lane_m >= base) & (lane_m < base + panel)
            for n in range(count):
                ph, plow = split2(pscr[pl.ds(n, panel, stride=pad), :])
                qh, qlow = split2(qscr[pl.ds(n, panel, stride=pad), :])
                right = jnp.concatenate([ph, plow, ph], axis=0)
                left = jnp.concatenate([qh, qh, qlow], axis=0)
                update = tdot(left, right)[:base]
                spot = pl.ds(n * size, base)
                m[spot, :] = jnp.where(inside, 0.0, m[spot, :]) - update


def inverse_kernel(factor, noise_ref, shift_ref, d_ref, e_ref, packed_ref, tail_ref, m, pscr, qscr):
    count, size, _ = noise_ref.shape
    half = size // 2
    pad = m.shape[0] // size
    row_full = lax.broadcasted_iota(jnp.int32, (size, size), 0)
    col_full = lax.broadcasted_iota(jnp.int32, (size, size), 1)
    on_diag = row_full == col_full
    for n in range(count):
        noise = noise_ref[n].astype(f32)
        d = (noise + noise.T) * (0.5 * factor)
        d = d + jnp.where(on_diag, shift_ref[pl.ds(n, 1), :], 0.0)
        d_ref[n] = d
        m[pl.ds(n * size, size), :] = d
        if n < pad - count:
            m[pl.ds((count + n) * size, size), :] = d
    eliminate(m, pscr, qscr, count, pad, size)
    row = lax.broadcasted_iota(jnp.int32, (half, half), 0)
    col = lax.broadcasted_iota(jnp.int32, (half, half), 1)
    tail_row = lax.broadcasted_iota(jnp.int32, (TAIL, size), 0)
    tile = jnp.zeros((TAIL, size), f32)
    for n in range(count):
        h, low = split2(m[pl.ds(n * size, size), :])
        e = tdot(jnp.concatenate([h, h, low], axis=0), jnp.concatenate([h, low, h], axis=0))
        e_ref[n] = e.astype(bf16)
        left = jnp.where(row >= col, e[:half, :half], e[half:, half:])
        packed_ref[n] = joined(left, e[:half, half:]).astype(bf16)
        diag = jnp.sum(jnp.where(on_diag, e, 0.0), axis=0, keepdims=True)
        tile = jnp.where(tail_row == n, diag, tile)
    tail_ref[...] = tile.astype(bf16)


def factor_kernel(
    capacity, scale, target_ref, rank_ref, near_ref, c_ref, d_ref, v_ref,
    k_ref, u_ref, out_ref, m, pscr, qscr,
):
    count, size, _ = d_ref.shape
    vec = v_ref.shape[0]
    half = size // 2
    pad = m.shape[0] // size
    row = lax.broadcasted_iota(jnp.int32, (half, half), 0)
    col = lax.broadcasted_iota(jnp.int32, (half, half), 1)
    tail_row = lax.broadcasted_iota(jnp.int32, (TAIL, size), 0)

    def schur(n, carry):
        fs, cs = [], []
        for k in range(3):
            t = target_ref[3 * n + k]
            c = rank_ref[3 * n + k]
            packed = near_ref[t, pl.ds(pl.multiple_of(c * half, half), half), :]
            packed = packed.astype(f32)
            tile = near_ref[t, pl.ds(capacity * half, TAIL), :].astype(f32)
            diag = jnp.sum(jnp.where(tail_row == c, tile, 0.0), axis=0, keepdims=True)
            flipped = packed.T
            part = packed[:, :half]
            part_t = flipped[:half, :]
            first = jnp.where(row >= col, part, part_t)
            last = jnp.where(row < col, part, part_t)
            last = jnp.where(row == col, diag[:, half:], last)
            inverse = jnp.concatenate(
                [joined(first, packed[:, half:]), joined(flipped[half:, :], last)], axis=0
            ).astype(bf16)
            coupling = c_ref[n, k]
            fs.append((dot_nn(coupling, inverse) * (scale * scale)).astype(bf16))
            cs.append(coupling)
        total = d_ref[n] - dot_nt(joined(*fs), joined(*cs))
        m[pl.ds(pl.multiple_of(n * size, size), size), :] = total
        return carry

    lax.fori_loop(0, count, schur, 0, unroll=7)
    for n in range(count, pad):
        m[pl.ds(n * size, size), :] = d_ref[0]
    eliminate(m, pscr, qscr, count, pad, size)
    out_ref[...] = jnp.zeros_like(out_ref)
    for n in range(count):
        k = m[pl.ds(n * size, size), :]
        k_ref[n] = k
        kh, kl = split2(k)
        vh, vl = split2(v_ref[:, n * size : (n + 1) * size])
        u = dot_nn(joined(vh, vh, vl), jnp.concatenate([kh, kl, kh], axis=0))
        u_ref[n] = u
        low = (u * scale).astype(bf16)
        for k in range(3):
            r = 3 * n + k
            spot = pl.ds(pl.multiple_of(rank_ref[r] * vec, vec), vec)
            out_ref[target_ref[r], spot, :] = dot_nn(low, c_ref[n, k]).astype(bf16)


def left_kernel(
    capacity, scale, target_ref, rank_ref, w_ref, u_ref, e_ref, c_ref,
    p_ref, left_ref, out_ref,
):
    count, vec, _ = u_ref.shape
    out_ref[...] = jnp.zeros_like(out_ref)
    for n in range(count):
        p = dot_nn(w_ref[pl.ds(n * vec, vec), :].astype(bf16), e_ref[n])
        p_ref[n] = p
        left_ref[n] = (u_ref[n] - p).astype(bf16)
        low = (p * scale).astype(bf16)
        for k in range(3):
            r = 3 * n + k
            spot = pl.ds(pl.multiple_of(rank_ref[r] * vec, vec), vec)
            out_ref[target_ref[r], spot, :] = dot_nn(low, c_ref[n, k]).astype(bf16)


def pulled(n, capacity, scale, target_ref, rank_ref, near_ref, c_ref):
    vec = near_ref.shape[1] // capacity
    got, cs = [], []
    for k in range(3):
        r = 3 * n + k
        spot = pl.ds(pl.multiple_of(rank_ref[r] * vec, vec), vec)
        got.append(near_ref[target_ref[r], spot, :])
        cs.append(c_ref[n, k])
    return scale * dot_nt(joined(*got), joined(*cs))


def middle_kernel(
    capacity, scale, target_ref, rank_ref, near_ref, pushed_ref, u_ref, p_ref, e_ref, d_ref, c_ref,
    t_ref, rest_ref,
):
    count, vec, _ = u_ref.shape
    for n in range(count):
        pushed = pushed_ref[pl.ds(n * vec, vec), :]
        q = pulled(n, capacity, scale, target_ref, rank_ref, near_ref, c_ref) - pushed
        t = p_ref[n] + dot_nn(q.astype(bf16), e_ref[n])
        t_ref[n] = t.astype(bf16)
        uh, ul = split2(u_ref[n])
        dh, dl = split2(d_ref[n])
        own = dot_nn(joined(uh, uh, ul), jnp.concatenate([dh, dl, dh], axis=0))
        rest_ref[n] = own - pushed


def final_kernel(capacity, scale, target_ref, rank_ref, near_ref, rest_ref, k_ref, c_ref, out_ref):
    count, size, _ = k_ref.shape
    for n in range(count):
        part = rest_ref[n] - pulled(n, capacity, scale, target_ref, rank_ref, near_ref, c_ref)
        ph, plow = split2(part)
        kh, kl = split2(k_ref[n])
        out_ref[:, n * size : (n + 1) * size] = dot_nt(
            joined(ph, ph, plow), joined(kh, kl, kh)
        )


def comm_kernel(geometry, pull, push, *refs):
    total, layers, capacity, count = geometry
    plane = total // layers
    refs = list(refs)
    take = lambda k: [refs.pop(0) for _ in range(k)]
    (table_ref,) = take(1)
    if pull:
        height, tail = pull
        parts = 2 if tail else 1
        own_ref = take(parts)
    if push:
        lanes_ref, out_ref = take(2)
    if pull:
        (near_ref,) = take(1)
    if push:
        (sum_ref,) = take(1)
    if pull:
        zbuf = [take(parts) for _ in range(layers - 1)]
        (send_ref,) = take(1)
    if push:
        arrive_ref, zout_ref, zin_ref = take(3)
    if pull:
        pz_send, pz_recv, pp_send, pp_recv = take(4)
    if push:
        sz_send, sz_recv, sp_send, sp_recv = take(4)
    me = lax.axis_index("rows")
    z = me // plane
    q = lax.rem(me, plane)
    zs = [jnp.bitwise_xor(z, o) for o in range(layers)]
    qs = [jnp.bitwise_xor(q, e) for e in range(plane)]

    barrier = pltpu.get_barrier_semaphore()
    partners = [zs[o] * plane + q for o in range(1, layers)]
    partners += [z * plane + qs[e] for e in range(1, plane)]
    for device in partners:
        pl.semaphore_signal(barrier, inc=1, device_id=(device,), device_id_type=MESH)

    def remote(src, dst, send, recv, device):
        return pltpu.make_async_remote_copy(
            src_ref=src, dst_ref=dst, send_sem=send, recv_sem=recv,
            device_id=(device,), device_id_type=MESH,
        )

    if pull:
        tail_row = lax.broadcasted_iota(jnp.int32, (TAIL, 128), 0)
        pull_z = [
            [
                remote(
                    own_ref[i], zbuf[o - 1][i], pz_send.at[o - 1, i], pz_recv.at[o - 1, i],
                    zs[o] * plane + q,
                )
                for i in range(parts)
            ]
            for o in range(1, layers)
        ]
        pull_p = {
            (o, e): remote(
                send_ref.at[o * plane + e], near_ref.at[zs[o] * plane + q],
                pp_send.at[o, e], pp_recv.at[o, e], z * plane + qs[e],
            )
            for o in range(layers)
            for e in range(1, plane)
        }

        def pack(o, e):
            source = own_ref if o == 0 else zbuf[o - 1]
            target, slot = (near_ref, zs[o] * plane + q) if e == 0 else (send_ref, o * plane + e)
            tile = jnp.zeros((TAIL, 128), f32)
            if tail:
                every = source[1][...].astype(f32)
            for c in range(capacity):
                index = jnp.maximum(table_ref[(qs[e] * layers + zs[o]) * capacity + c], 0)
                target[slot, pl.ds(c * height, height), :] = source[0][index]
                if tail:
                    line = jnp.sum(jnp.where(tail_row == index, every, 0.0), axis=0, keepdims=True)
                    tile = jnp.where(tail_row == c, line, tile)
            if tail:
                target[slot, pl.ds(capacity * height, TAIL), :] = tile.astype(bf16)

        for e in range(1, plane):
            pack(0, e)
    if push:
        step = out_ref.shape[1]
        vec = step // capacity
        width = plane * step
        push_p = {
            (o, e): remote(
                out_ref.at[zs[o] * plane + qs[e]], arrive_ref.at[zs[o], pl.ds(pl.multiple_of(q * step, step), step)],
                sp_send.at[o, e], sp_recv.at[o, e], z * plane + qs[e],
            )
            for o in range(layers)
            for e in range(1, plane)
        }
        push_z = [
            remote(zout_ref.at[o - 1], zin_ref.at[o - 1], sz_send.at[o - 1], sz_recv.at[o - 1], zs[o] * plane + q)
            for o in range(1, layers)
        ]

        def gather_sum(o):
            lanes = lanes_ref[pl.ds(zs[o], 1), :]
            row = lax.broadcasted_iota(jnp.int32, (vec, width), 0)
            col = lax.broadcasted_iota(jnp.int32, (vec, width), 1)
            same = row == lax.rem(col, vec)
            pick = jnp.concatenate(
                [jnp.where(same & (lanes == k), 1.0, 0.0).astype(bf16) for k in range(count)], axis=0
            )
            return dot_nn(pick, arrive_ref[zs[o]])

    pl.semaphore_wait(barrier, len(partners))
    if pull:
        for o in reversed(range(1, layers)):
            for copy in pull_z[o - 1]:
                copy.start()
    if push:
        for o in list(range(1, layers)) + [0]:
            for e in reversed(range(1, plane)):
                push_p[o, e].start()
        for o in range(layers):
            here = pl.ds(pl.multiple_of(q * step, step), step)
            arrive_ref[zs[o], here, :] = out_ref[zs[o] * plane + q]
    if pull:
        for e in reversed(range(1, plane)):
            pull_p[0, e].start()
        pack(0, 0)
    for o in range(1, layers):
        if push:
            for e in range(1, plane):
                push_p[o, e].wait_recv()
            zout_ref[o - 1] = gather_sum(o).astype(bf16)
            push_z[o - 1].start()
        if pull:
            for copy in pull_z[o - 1]:
                copy.wait_recv()
            for e in reversed(range(1, plane)):
                pack(o, e)
                pull_p[o, e].start()
            pack(o, 0)
    if push:
        for e in range(1, plane):
            push_p[0, e].wait_recv()
        total_sum = gather_sum(0)
        for o in range(1, layers):
            push_z[o - 1].wait_recv()
            total_sum = total_sum + zin_ref[o - 1].astype(f32)
        sum_ref[...] = total_sum
        for o in range(1, layers):
            push_z[o - 1].wait_send()
        for copy in push_p.values():
            copy.wait_send()
    if pull:
        for copy in pull_p.values():
            copy.wait_recv()
        for copy in pull_p.values():
            copy.wait_send()
        for copies in pull_z:
            for copy in copies:
                copy.wait_send()


def communicate(geometry, number, table, pull=None, own=None, push=None, lanes=None):
    total, layers, capacity, count = geometry
    plane = total // layers
    smem = pl.BlockSpec(memory_space=pltpu.SMEM)
    vmem = pl.BlockSpec(memory_space=pltpu.VMEM)
    args, specs, shapes, scratch, sems = [table], [smem], [], [], []
    dma = pltpu.SemaphoreType.DMA
    if pull:
        args += own
        specs += [vmem] * len(own)
        height, tail = pull
        block = (capacity * height + tail, own[0].shape[-1])
        shapes += [jax.ShapeDtypeStruct((total,) + block, bf16)]
        scratch += [pltpu.VMEM(part.shape, bf16) for part in own] * (layers - 1)
        scratch += [pltpu.VMEM((total,) + block, bf16)]
        sems += [dma((layers - 1, len(own)))] * 2 + [dma((layers, plane))] * 2
    if push is not None:
        args += [lanes, push]
        specs += [vmem, vmem]
        step, size = push.shape[1:]
        height = step // capacity * count
        shapes += [jax.ShapeDtypeStruct((height, size), f32)]
        scratch += [pltpu.VMEM((layers, plane * step, size), push.dtype)]
        scratch += [pltpu.VMEM((layers - 1, height, size), push.dtype)] * 2
        sems += [dma((layers - 1,))] * 2 + [dma((layers, plane))] * 2
    return pl.pallas_call(
        functools.partial(comm_kernel, geometry, pull, push is not None),
        out_shape=shapes,
        in_specs=specs,
        out_specs=[vmem] * len(shapes),
        scratch_shapes=scratch + sems,
        compiler_params=pltpu.CompilerParams(collective_id=number, has_side_effects=True),
    )(*args)


def call(kernel, scalars, arrays, shapes, scratch=()):
    smem = pl.BlockSpec(memory_space=pltpu.SMEM)
    vmem = pl.BlockSpec(memory_space=pltpu.VMEM)
    return pl.pallas_call(
        kernel,
        out_shape=[jax.ShapeDtypeStruct(shape, dtype) for shape, dtype in shapes],
        in_specs=[smem] * len(scalars) + [vmem] * len(arrays),
        out_specs=[vmem] * len(shapes),
        scratch_shapes=[pltpu.VMEM(shape, f32) for shape in scratch],
    )(*scalars, *arrays)


def body(diag_noise, couplings, shifts, near_devices, near_slots, vectors):
    dev_count = lax.axis_size("rows")
    my_index = lax.axis_index("rows")
    row_count, block_size = diag_noise.shape[:2]
    vec_count = vectors.shape[0]
    capacity = 3 * row_count // (dev_count - 1) + 2
    layers = LAYERS
    plane = dev_count // layers
    factor = 0.5 / math.sqrt(block_size)
    scale = 0.4 / math.sqrt(block_size)
    geometry = (dev_count, layers, capacity, row_count)

    target = ((my_index - 1 - near_devices) % dev_count).reshape(-1)
    device_onehot = (target[:, None] == jnp.arange(dev_count, dtype=jnp.int32)[None, :]).astype(
        jnp.int32
    )
    running = jnp.cumsum(device_onehot, axis=0) - 1
    rank = jnp.sum(running * device_onehot, axis=1)
    position = (target % plane * layers + target // plane) * capacity + rank
    hit = position[None, :] == jnp.arange(dev_count * capacity, dtype=jnp.int32)[:, None]
    asked = jnp.sum(jnp.where(hit, near_slots.reshape(1, -1) + 1, 0), axis=1) - 1
    groups = [[i * plane + j for j in range(plane)] for i in range(layers)]
    table = lax.all_to_all(
        asked.reshape(plane, layers * capacity), "rows", 0, 0,
        axis_index_groups=groups, tiled=True,
    ).reshape(-1)
    lanes = table.reshape(plane, layers, capacity).transpose(1, 0, 2)
    lanes = jnp.repeat(lanes.reshape(layers, -1), vec_count, axis=1)

    half = block_size // 2
    pad = -(-row_count // 8) * 8
    work = ((pad * block_size, block_size),) + ((PANEL * pad, block_size),) * 2
    block_shape = (row_count, block_size, block_size)
    rows_shape = (row_count, vec_count, block_size)
    out_shape = (dev_count, capacity * vec_count, block_size)
    diag_own, inverse, packed, tails = call(
        functools.partial(inverse_kernel, factor),
        (),
        (diag_noise, shifts.astype(f32)),
        (
            (block_shape, f32),
            (block_shape, bf16),
            ((row_count, half, block_size), bf16),
            ((TAIL, block_size), bf16),
        ),
        work,
    )
    (near,) = communicate(geometry, 0, table, pull=(half, TAIL), own=[packed, tails])
    k_all, u, outgoing = call(
        functools.partial(factor_kernel, capacity, scale),
        (target, rank),
        (near, couplings, diag_own, vectors),
        ((block_shape, f32), (rows_shape, f32), (out_shape, bf16)),
        work,
    )
    (w,) = communicate(geometry, 1, table, push=outgoing, lanes=lanes)
    p, left, outgoing = call(
        functools.partial(left_kernel, capacity, scale),
        (target, rank),
        (w, u, inverse, couplings),
        ((rows_shape, f32), (rows_shape, bf16), (out_shape, bf16)),
    )
    near, pushed = communicate(
        geometry, 2, table, pull=(vec_count, 0), own=[left], push=outgoing, lanes=lanes
    )
    t, rest = call(
        functools.partial(middle_kernel, capacity, scale),
        (target, rank),
        (near, pushed, u, p, inverse, diag_own, couplings),
        ((rows_shape, bf16), (rows_shape, f32)),
    )
    (near,) = communicate(geometry, 3, table, pull=(vec_count, 0), own=[t])
    (result,) = call(
        functools.partial(final_kernel, capacity, scale),
        (target, rank),
        (near, rest, k_all, couplings),
        ((vectors.shape, f32),),
    )
    return result


def solution(mesh):
    return jax.shard_map(
        body,
        mesh=mesh,
        in_specs=(
            P("rows", None, None),
            P("rows", None, None, None),
            P("rows", None),
            P("rows", None),
            P("rows", None),
            P(None, "rows"),
        ),
        out_specs=P(None, "rows"),
        check_vma=False,
    )
```

```python
import functools
import math

import jax
import jax.numpy as jnp
from jax import lax
from jax.experimental import pallas as pl
from jax.experimental.pallas import tpu as pltpu
from jax.sharding import PartitionSpec as P

PANEL = 16
GROUP = 4
LAYERS = 4
TAIL = 16
MESH = pl.DeviceIdType.MESH
bf16, f32 = jnp.bfloat16, jnp.float32


def split2(x):
    high = x.astype(bf16)
    return high, (x - high.astype(f32)).astype(bf16)


def joined(*parts):
    return jnp.concatenate(parts, axis=-1)


def tdot(a, b):
    return lax.dot_general(a, b, (((0,), (0,)), ((), ())), preferred_element_type=f32)


def dot_nn(a, b):
    return jnp.dot(a, b, preferred_element_type=f32)


def dot_nt(a, b):
    return lax.dot_general(a, b, (((1,), (1,)), ((), ())), preferred_element_type=f32)


def eliminate(m, pscr, qscr, count, pad, size):
    panel = PANEL
    lane = lax.broadcasted_iota(jnp.int32, (pad, size), 1)
    for block in reversed(range(size // panel)):
        base = block * panel
        rows = [m[pl.ds(base + r, pad, stride=size), :] for r in range(panel)]
        for k in reversed(range(panel)):
            col = base + k
            here = lane == col
            if (k + 1) % GROUP == 0:
                first = k + 1 - GROUP
                tile = {
                    (i, c): jnp.broadcast_to(rows[i][:, base + c : base + c + 1], (pad, size))
                    for c in range(first, k + 1)
                    for i in range(c + 1)
                }
            inv = 1.0 / tile[k, k]
            for c in reversed(range(first, k)):
                ratio = tile[c, k] * inv
                for i in range(c + 1):
                    tile[i, c] = tile[i, c] - tile[i, k] * ratio
            pivot_row = jnp.where(here, 1.0, rows[k])
            scaled = pivot_row * inv
            for i in range(k):
                rows[i] = jnp.where(here, 0.0, rows[i]) - tile[i, k] * scaled
            if block:
                pscr[pl.ds(k * pad, pad), :] = jnp.where(
                    (lane >= base) & (lane < col), 0.0, pivot_row
                )
                qscr[pl.ds(k * pad, pad), :] = scaled
            m[pl.ds(col, pad, stride=size), :] = jnp.where(
                lane >= col, pivot_row * jnp.sqrt(inv), 0.0
            )
        if block:
            lane_m = lax.broadcasted_iota(jnp.int32, (base, size), 1)
            inside = (lane_m >= base) & (lane_m < base + panel)
            for n in range(count):
                ph, plow = split2(pscr[pl.ds(n, panel, stride=pad), :])
                qh, qlow = split2(qscr[pl.ds(n, panel, stride=pad), :])
                right = jnp.concatenate([ph, plow, ph], axis=0)
                left = jnp.concatenate([qh, qh, qlow], axis=0)
                update = tdot(left, right)[:base]
                spot = pl.ds(n * size, base)
                m[spot, :] = jnp.where(inside, 0.0, m[spot, :]) - update


def inverse_kernel(factor, noise_ref, shift_ref, d_ref, e_ref, packed_ref, tail_ref, m, pscr, qscr):
    count, size, _ = noise_ref.shape
    half = size // 2
    pad = m.shape[0] // size
    row_full = lax.broadcasted_iota(jnp.int32, (size, size), 0)
    col_full = lax.broadcasted_iota(jnp.int32, (size, size), 1)
    on_diag = row_full == col_full
    for n in range(count):
        noise = noise_ref[n].astype(f32)
        d = (noise + noise.T) * (0.5 * factor)
        d = d + jnp.where(on_diag, shift_ref[pl.ds(n, 1), :], 0.0)
        d_ref[n] = d
        m[pl.ds(n * size, size), :] = d
        if n < pad - count:
            m[pl.ds((count + n) * size, size), :] = d
    eliminate(m, pscr, qscr, count, pad, size)
    row = lax.broadcasted_iota(jnp.int32, (half, half), 0)
    col = lax.broadcasted_iota(jnp.int32, (half, half), 1)
    tail_row = lax.broadcasted_iota(jnp.int32, (TAIL, size), 0)
    tile = jnp.zeros((TAIL, size), f32)
    for n in range(count):
        h, low = split2(m[pl.ds(n * size, size), :])
        e = tdot(jnp.concatenate([h, h, low], axis=0), jnp.concatenate([h, low, h], axis=0))
        e_ref[n] = e.astype(bf16)
        left = jnp.where(row >= col, e[:half, :half], e[half:, half:])
        packed_ref[n] = joined(left, e[:half, half:]).astype(bf16)
        diag = jnp.sum(jnp.where(on_diag, e, 0.0), axis=0, keepdims=True)
        tile = jnp.where(tail_row == n, diag, tile)
    tail_ref[...] = tile.astype(bf16)


def factor_kernel(
    capacity, scale, target_ref, rank_ref, near_ref, c_ref, d_ref, v_ref,
    k_ref, u_ref, out_ref, m, pscr, qscr,
):
    count, size, _ = d_ref.shape
    vec = v_ref.shape[0]
    half = size // 2
    pad = m.shape[0] // size
    row = lax.broadcasted_iota(jnp.int32, (half, half), 0)
    col = lax.broadcasted_iota(jnp.int32, (half, half), 1)
    tail_row = lax.broadcasted_iota(jnp.int32, (TAIL, size), 0)

    def schur(n, carry):
        fs, cs = [], []
        for k in range(3):
            t = target_ref[3 * n + k]
            c = rank_ref[3 * n + k]
            packed = near_ref[t, pl.ds(pl.multiple_of(c * half, half), half), :]
            packed = packed.astype(f32)
            tile = near_ref[t, pl.ds(capacity * half, TAIL), :].astype(f32)
            diag = jnp.sum(jnp.where(tail_row == c, tile, 0.0), axis=0, keepdims=True)
            flipped = packed.T
            part = packed[:, :half]
            part_t = flipped[:half, :]
            first = jnp.where(row >= col, part, part_t)
            last = jnp.where(row < col, part, part_t)
            last = jnp.where(row == col, diag[:, half:], last)
            inverse = jnp.concatenate(
                [joined(first, packed[:, half:]), joined(flipped[half:, :], last)], axis=0
            ).astype(bf16)
            coupling = c_ref[n, k]
            fs.append((dot_nn(coupling, inverse) * (scale * scale)).astype(bf16))
            cs.append(coupling)
        total = d_ref[n] - dot_nt(joined(*fs), joined(*cs))
        m[pl.ds(pl.multiple_of(n * size, size), size), :] = total
        return carry

    lax.fori_loop(0, count, schur, 0, unroll=7)
    for n in range(count, pad):
        m[pl.ds(n * size, size), :] = d_ref[0]
    eliminate(m, pscr, qscr, count, pad, size)
    out_ref[...] = jnp.zeros_like(out_ref)
    for n in range(count):
        k = m[pl.ds(n * size, size), :]
        k_ref[n] = k
        kh, kl = split2(k)
        vh, vl = split2(v_ref[:, n * size : (n + 1) * size])
        u = dot_nn(joined(vh, vh, vl), jnp.concatenate([kh, kl, kh], axis=0))
        u_ref[n] = u
        low = (u * scale).astype(bf16)
        for k in range(3):
            r = 3 * n + k
            spot = pl.ds(pl.multiple_of(rank_ref[r] * vec, vec), vec)
            out_ref[target_ref[r], spot, :] = dot_nn(low, c_ref[n, k]).astype(bf16)


def left_kernel(
    capacity, scale, target_ref, rank_ref, w_ref, u_ref, e_ref, c_ref,
    p_ref, left_ref, out_ref,
):
    count, vec, _ = u_ref.shape
    out_ref[...] = jnp.zeros_like(out_ref)
    for n in range(count):
        p = dot_nn(w_ref[pl.ds(n * vec, vec), :].astype(bf16), e_ref[n])
        p_ref[n] = p
        left_ref[n] = (u_ref[n] - p).astype(bf16)
        low = (p * scale).astype(bf16)
        for k in range(3):
            r = 3 * n + k
            spot = pl.ds(pl.multiple_of(rank_ref[r] * vec, vec), vec)
            out_ref[target_ref[r], spot, :] = dot_nn(low, c_ref[n, k]).astype(bf16)


def pulled(n, capacity, scale, target_ref, rank_ref, near_ref, c_ref):
    vec = near_ref.shape[1] // capacity
    got, cs = [], []
    for k in range(3):
        r = 3 * n + k
        spot = pl.ds(pl.multiple_of(rank_ref[r] * vec, vec), vec)
        got.append(near_ref[target_ref[r], spot, :])
        cs.append(c_ref[n, k])
    return scale * dot_nt(joined(*got), joined(*cs))


def middle_kernel(
    capacity, scale, target_ref, rank_ref, near_ref, pushed_ref, u_ref, p_ref, e_ref, d_ref, c_ref,
    t_ref, rest_ref,
):
    count, vec, _ = u_ref.shape
    for n in range(count):
        pushed = pushed_ref[pl.ds(n * vec, vec), :]
        q = pulled(n, capacity, scale, target_ref, rank_ref, near_ref, c_ref) - pushed
        t = p_ref[n] + dot_nn(q.astype(bf16), e_ref[n])
        t_ref[n] = t.astype(bf16)
        uh, ul = split2(u_ref[n])
        dh, dl = split2(d_ref[n])
        own = dot_nn(joined(uh, uh, ul), jnp.concatenate([dh, dl, dh], axis=0))
        rest_ref[n] = own - pushed


def final_kernel(capacity, scale, target_ref, rank_ref, near_ref, rest_ref, k_ref, c_ref, out_ref):
    count, size, _ = k_ref.shape
    for n in range(count):
        part = rest_ref[n] - pulled(n, capacity, scale, target_ref, rank_ref, near_ref, c_ref)
        ph, plow = split2(part)
        kh, kl = split2(k_ref[n])
        out_ref[:, n * size : (n + 1) * size] = dot_nt(
            joined(ph, ph, plow), joined(kh, kl, kh)
        )


def comm_kernel(geometry, pull, push, *refs):
    total, layers, capacity, count = geometry
    plane = total // layers
    refs = list(refs)
    take = lambda k: [refs.pop(0) for _ in range(k)]
    (table_ref,) = take(1)
    if pull:
        height, tail = pull
        parts = 2 if tail else 1
        own_ref = take(parts)
    if push:
        lanes_ref, out_ref = take(2)
    if pull:
        (near_ref,) = take(1)
    if push:
        (sum_ref,) = take(1)
    if pull:
        relayed = {(d, s): take(parts) for d in (-1, 1) for s in range(layers - 1)}
        (send_ref,) = take(1)
    if push:
        arrive_ref, zout_ref, zin_ref = take(3)
    if pull:
        pz_send, pz_recv, pp_send, pp_recv = take(4)
    if push:
        sz_send, sz_recv, sp_send, sp_recv = take(4)
    me = lax.axis_index("rows")
    z = me // plane
    q = lax.rem(me, plane)
    zs = [jnp.bitwise_xor(z, o) for o in range(layers)]
    qs = [jnp.bitwise_xor(q, e) for e in range(plane)]

    barrier = pltpu.get_barrier_semaphore()
    partners = [zs[o] * plane + q for o in range(1, layers)]
    partners += [z * plane + qs[e] for e in range(1, plane)]
    for device in partners:
        pl.semaphore_signal(barrier, inc=1, device_id=(device,), device_id_type=MESH)

    def remote(src, dst, send, recv, device):
        return pltpu.make_async_remote_copy(
            src_ref=src, dst_ref=dst, send_sem=send, recv_sem=recv,
            device_id=(device,), device_id_type=MESH,
        )

    if pull:
        tail_row = lax.broadcasted_iota(jnp.int32, (TAIL, 128), 0)

        def held(d, s):
            return own_ref if s < 0 else relayed[d, s]

        def hop(d, s):
            side = 0 if d < 0 else 1
            there = jnp.clip(z - d, 0, layers - 1)
            return [
                remote(
                    held(d, s - 1)[i], relayed[d, s][i], pz_send.at[side, s, i],
                    pz_recv.at[side, s, i], there * plane + q,
                )
                for i in range(parts)
            ]

        def inside(x):
            return (x >= 0) & (x < layers)

        def spread(d, s, e):
            layer = z if s < 0 else jnp.clip(z + d * (s + 1), 0, layers - 1)
            return remote(
                send_ref.at[layer, e], near_ref.at[layer * plane + q],
                pp_send.at[layer, e], pp_recv.at[layer, e], z * plane + qs[e],
            )

        def pack(d, s, e):
            source = held(d, s)
            layer = z if s < 0 else jnp.clip(z + d * (s + 1), 0, layers - 1)
            tile = jnp.zeros((TAIL, 128), f32)
            if tail:
                every = source[1][...].astype(f32)

            def put(rows, value):
                if e == 0:
                    near_ref[layer * plane + q, rows, :] = value
                else:
                    send_ref[layer, e, rows, :] = value

            for c in range(capacity):
                index = jnp.maximum(table_ref[(qs[e] * layers + layer) * capacity + c], 0)
                put(pl.ds(c * height, height), source[0][index])
                if tail:
                    line = jnp.sum(jnp.where(tail_row == index, every, 0.0), axis=0, keepdims=True)
                    tile = jnp.where(tail_row == c, line, tile)
            if tail:
                put(pl.ds(capacity * height, TAIL), tile.astype(bf16))

        def serve(d, s):
            for e in reversed(range(plane)):
                pack(d, s, e)
                if e:
                    spread(d, s, e).start()

        def advance(d, s):
            @pl.when(inside(z + d * (s + 1)))
            def _():
                for copy in hop(d, s):
                    copy.wait_recv()
            if s < layers - 2:
                @pl.when(inside(z + d * (s + 1)) & inside(z - d))
                def _():
                    for copy in hop(d, s + 1):
                        copy.start()

            @pl.when(inside(z + d * (s + 1)))
            def _():
                serve(d, s)

    if push:
        step = out_ref.shape[1]
        vec = step // capacity
        width = plane * step
        push_p = {
            (o, e): remote(
                out_ref.at[zs[o] * plane + qs[e]], arrive_ref.at[zs[o], pl.ds(pl.multiple_of(q * step, step), step)],
                sp_send.at[o, e], sp_recv.at[o, e], z * plane + qs[e],
            )
            for o in range(layers)
            for e in range(1, plane)
        }
        push_z = [
            remote(zout_ref.at[o - 1], zin_ref.at[o - 1], sz_send.at[o - 1], sz_recv.at[o - 1], zs[o] * plane + q)
            for o in range(1, layers)
        ]

        def gather_sum(o):
            lanes = lanes_ref[pl.ds(zs[o], 1), :]
            row = lax.broadcasted_iota(jnp.int32, (vec, width), 0)
            col = lax.broadcasted_iota(jnp.int32, (vec, width), 1)
            same = row == lax.rem(col, vec)
            pick = jnp.concatenate(
                [jnp.where(same & (lanes == k), 1.0, 0.0).astype(bf16) for k in range(count)], axis=0
            )
            return dot_nn(pick, arrive_ref[zs[o]])

    far_first = list(reversed(range(1, layers)))
    pl.semaphore_wait(barrier, len(partners))
    if pull:
        for d in (-1, 1):
            @pl.when(inside(z - d))
            def _():
                for copy in hop(d, 0):
                    copy.start()
    if push:
        for o in far_first + [0]:
            for e in reversed(range(1, plane)):
                push_p[o, e].start()
    if pull:
        serve(0, -1)
    if push:
        for o in range(layers):
            here = pl.ds(pl.multiple_of(q * step, step), step)
            arrive_ref[zs[o], here, :] = out_ref[zs[o] * plane + q]
    for i, o in enumerate(far_first):
        if push:
            for e in range(1, plane):
                push_p[o, e].wait_recv()
            zout_ref[o - 1] = gather_sum(o).astype(bf16)
            push_z[o - 1].start()
        if pull:
            advance(-1, i)
            advance(1, i)
    if push:
        for e in range(1, plane):
            push_p[0, e].wait_recv()
        total_sum = gather_sum(0)
        for o in far_first:
            push_z[o - 1].wait_recv()
            total_sum = total_sum + zin_ref[o - 1].astype(f32)
        sum_ref[...] = total_sum
        for o in range(1, layers):
            push_z[o - 1].wait_send()
        for copy in push_p.values():
            copy.wait_send()
    if pull:
        for d in (-1, 1):
            for s in range(layers - 1):
                @pl.when(inside(z - d) & inside(z + d * s))
                def _():
                    for copy in hop(d, s):
                        copy.wait_send()
        for layer in range(layers):
            for e in range(1, plane):
                copy = remote(
                    send_ref.at[layer, e], near_ref.at[layer * plane + q],
                    pp_send.at[layer, e], pp_recv.at[layer, e], z * plane + qs[e],
                )
                copy.wait_recv()
                copy.wait_send()


def communicate(geometry, number, table, pull=None, own=None, push=None, lanes=None):
    total, layers, capacity, count = geometry
    plane = total // layers
    smem = pl.BlockSpec(memory_space=pltpu.SMEM)
    vmem = pl.BlockSpec(memory_space=pltpu.VMEM)
    args, specs, shapes, scratch, sems = [table], [smem], [], [], []
    dma = pltpu.SemaphoreType.DMA
    if pull:
        args += own
        specs += [vmem] * len(own)
        height, tail = pull
        block = (capacity * height + tail, own[0].shape[-1])
        shapes += [jax.ShapeDtypeStruct((total,) + block, bf16)]
        scratch += [pltpu.VMEM(part.shape, bf16) for part in own] * (2 * layers - 2)
        scratch += [pltpu.VMEM((layers, plane) + block, bf16)]
        sems += [dma((2, layers - 1, len(own)))] * 2 + [dma((layers, plane))] * 2
    if push is not None:
        args += [lanes, push]
        specs += [vmem, vmem]
        step, size = push.shape[1:]
        height = step // capacity * count
        shapes += [jax.ShapeDtypeStruct((height, size), f32)]
        scratch += [pltpu.VMEM((layers, plane * step, size), push.dtype)]
        scratch += [pltpu.VMEM((layers - 1, height, size), push.dtype)] * 2
        sems += [dma((layers - 1,))] * 2 + [dma((layers, plane))] * 2
    return pl.pallas_call(
        functools.partial(comm_kernel, geometry, pull, push is not None),
        out_shape=shapes,
        in_specs=specs,
        out_specs=[vmem] * len(shapes),
        scratch_shapes=scratch + sems,
        compiler_params=pltpu.CompilerParams(collective_id=number, has_side_effects=True),
    )(*args)


def call(kernel, scalars, arrays, shapes, scratch=()):
    smem = pl.BlockSpec(memory_space=pltpu.SMEM)
    vmem = pl.BlockSpec(memory_space=pltpu.VMEM)
    return pl.pallas_call(
        kernel,
        out_shape=[jax.ShapeDtypeStruct(shape, dtype) for shape, dtype in shapes],
        in_specs=[smem] * len(scalars) + [vmem] * len(arrays),
        out_specs=[vmem] * len(shapes),
        scratch_shapes=[pltpu.VMEM(shape, f32) for shape in scratch],
    )(*scalars, *arrays)


def body(diag_noise, couplings, shifts, near_devices, near_slots, vectors):
    dev_count = lax.axis_size("rows")
    my_index = lax.axis_index("rows")
    row_count, block_size = diag_noise.shape[:2]
    vec_count = vectors.shape[0]
    capacity = 3 * row_count // (dev_count - 1) + 2
    layers = LAYERS
    plane = dev_count // layers
    factor = 0.5 / math.sqrt(block_size)
    scale = 0.4 / math.sqrt(block_size)
    geometry = (dev_count, layers, capacity, row_count)

    target = ((my_index - 1 - near_devices) % dev_count).reshape(-1)
    device_onehot = (target[:, None] == jnp.arange(dev_count, dtype=jnp.int32)[None, :]).astype(
        jnp.int32
    )
    running = jnp.cumsum(device_onehot, axis=0) - 1
    rank = jnp.sum(running * device_onehot, axis=1)
    position = (target % plane * layers + target // plane) * capacity + rank
    hit = position[None, :] == jnp.arange(dev_count * capacity, dtype=jnp.int32)[:, None]
    asked = jnp.sum(jnp.where(hit, near_slots.reshape(1, -1) + 1, 0), axis=1) - 1
    groups = [[i * plane + j for j in range(plane)] for i in range(layers)]
    table = lax.all_to_all(
        asked.reshape(plane, layers * capacity), "rows", 0, 0,
        axis_index_groups=groups, tiled=True,
    ).reshape(-1)
    lanes = table.reshape(plane, layers, capacity).transpose(1, 0, 2)
    lanes = jnp.repeat(lanes.reshape(layers, -1), vec_count, axis=1)

    half = block_size // 2
    pad = -(-row_count // 8) * 8
    work = ((pad * block_size, block_size),) + ((PANEL * pad, block_size),) * 2
    block_shape = (row_count, block_size, block_size)
    rows_shape = (row_count, vec_count, block_size)
    out_shape = (dev_count, capacity * vec_count, block_size)
    diag_own, inverse, packed, tails = call(
        functools.partial(inverse_kernel, factor),
        (),
        (diag_noise, shifts.astype(f32)),
        (
            (block_shape, f32),
            (block_shape, bf16),
            ((row_count, half, block_size), bf16),
            ((TAIL, block_size), bf16),
        ),
        work,
    )
    (near,) = communicate(geometry, 0, table, pull=(half, TAIL), own=[packed, tails])
    k_all, u, outgoing = call(
        functools.partial(factor_kernel, capacity, scale),
        (target, rank),
        (near, couplings, diag_own, vectors),
        ((block_shape, f32), (rows_shape, f32), (out_shape, bf16)),
        work,
    )
    (w,) = communicate(geometry, 1, table, push=outgoing, lanes=lanes)
    p, left, outgoing = call(
        functools.partial(left_kernel, capacity, scale),
        (target, rank),
        (w, u, inverse, couplings),
        ((rows_shape, f32), (rows_shape, bf16), (out_shape, bf16)),
    )
    near, pushed = communicate(
        geometry, 2, table, pull=(vec_count, 0), own=[left], push=outgoing, lanes=lanes
    )
    t, rest = call(
        functools.partial(middle_kernel, capacity, scale),
        (target, rank),
        (near, pushed, u, p, inverse, diag_own, couplings),
        ((rows_shape, bf16), (rows_shape, f32)),
    )
    (near,) = communicate(geometry, 3, table, pull=(vec_count, 0), own=[t])
    (result,) = call(
        functools.partial(final_kernel, capacity, scale),
        (target, rank),
        (near, rest, k_all, couplings),
        ((vectors.shape, f32),),
    )
    return result


def solution(mesh):
    return jax.shard_map(
        body,
        mesh=mesh,
        in_specs=(
            P("rows", None, None),
            P("rows", None, None, None),
            P("rows", None),
            P("rows", None),
            P("rows", None),
            P(None, "rows"),
        ),
        out_specs=P(None, "rows"),
        check_vma=False,
    )
```

```python
import functools
import math

import jax
import jax.numpy as jnp
from jax import lax
from jax.experimental import pallas as pl
from jax.experimental.pallas import tpu as pltpu
from jax.sharding import PartitionSpec as P

PANEL = 16
GROUP = 4
LAYERS = 4
TAIL = 16
UNROLL = 7
MESH = pl.DeviceIdType.MESH
bf16, f32 = jnp.bfloat16, jnp.float32


def split2(x):
    high = x.astype(bf16)
    return high, (x - high.astype(f32)).astype(bf16)


def joined(*parts):
    return jnp.concatenate(parts, axis=-1)


def tdot(a, b):
    return lax.dot_general(a, b, (((0,), (0,)), ((), ())), preferred_element_type=f32)


def dot_nn(a, b):
    return jnp.dot(a, b, preferred_element_type=f32)


def dot_nt(a, b):
    return lax.dot_general(a, b, (((1,), (1,)), ((), ())), preferred_element_type=f32)


def eliminate(m, pscr, qscr, count, pad, size):
    panel = PANEL
    lane = lax.broadcasted_iota(jnp.int32, (pad, size), 1)
    for block in reversed(range(size // panel)):
        base = block * panel
        rows = [m[pl.ds(base + r, pad, stride=size), :] for r in range(panel)]
        for k in reversed(range(panel)):
            col = base + k
            here = lane == col
            if (k + 1) % GROUP == 0:
                first = k + 1 - GROUP
                tile = {
                    (i, c): jnp.broadcast_to(rows[i][:, base + c : base + c + 1], (pad, size))
                    for c in range(first, k + 1)
                    for i in range(c + 1)
                }
            inv = 1.0 / tile[k, k]
            for c in reversed(range(first, k)):
                ratio = tile[c, k] * inv
                for i in range(c + 1):
                    tile[i, c] = tile[i, c] - tile[i, k] * ratio
            pivot_row = jnp.where(here, 1.0, rows[k])
            scaled = pivot_row * inv
            for i in range(k):
                rows[i] = jnp.where(here, 0.0, rows[i]) - tile[i, k] * scaled
            if block:
                pscr[pl.ds(k * pad, pad), :] = jnp.where(
                    (lane >= base) & (lane < col), 0.0, pivot_row
                )
                qscr[pl.ds(k * pad, pad), :] = scaled
            m[pl.ds(col, pad, stride=size), :] = jnp.where(
                lane >= col, pivot_row * jnp.sqrt(inv), 0.0
            )
        if block:
            lane_m = lax.broadcasted_iota(jnp.int32, (base, size), 1)
            inside = (lane_m >= base) & (lane_m < base + panel)
            for n in range(count):
                ph, plow = split2(pscr[pl.ds(n, panel, stride=pad), :])
                qh, qlow = split2(qscr[pl.ds(n, panel, stride=pad), :])
                right = jnp.concatenate([ph, plow, ph], axis=0)
                left = jnp.concatenate([qh, qh, qlow], axis=0)
                update = tdot(left, right)[:base]
                spot = pl.ds(n * size, base)
                m[spot, :] = jnp.where(inside, 0.0, m[spot, :]) - update


def inside(x, layers):
    return (x >= 0) & (x < layers)


class Links:
    def __init__(self, total, layers):
        self.layers, self.plane = layers, total // layers
        me = lax.axis_index("rows")
        self.z = me // self.plane
        self.q = lax.rem(me, self.plane)
        self.zs = [jnp.bitwise_xor(self.z, o) for o in range(layers)]
        self.qs = [jnp.bitwise_xor(self.q, e) for e in range(self.plane)]

    def partners(self):
        far = [self.zs[o] * self.plane + self.q for o in range(1, self.layers)]
        return far + [self.z * self.plane + self.qs[e] for e in range(1, self.plane)]

    def remote(self, src, dst, send, recv, device):
        return pltpu.make_async_remote_copy(
            src_ref=src, dst_ref=dst, send_sem=send, recv_sem=recv,
            device_id=(device,), device_id_type=MESH,
        )


class Pull:
    def __init__(self, links, table_ref, capacity, count, tail, refs):
        self.links, self.table, self.capacity, self.tail = links, table_ref, capacity, tail
        self.own, self.send, self.near, *rest = refs
        moves = [(d, s) for s in range(links.layers - 1) for d in (-1, 1)]
        self.relayed = dict(zip(moves, rest))
        self.z_send, self.z_recv, self.p_send, self.p_recv = rest[len(moves):]
        self.tiles = (self.own.shape[0] - tail) // count
        self.last = count * self.tiles
        self.group = capacity * self.tiles + tail

    def held(self, d, s):
        return self.own if s < 0 else self.relayed[d, s]

    def layer(self, d, s):
        return self.links.z if s < 0 else jnp.clip(self.links.z + d * (s + 1), 0, self.links.layers - 1)

    def hop(self, d, s):
        k = self.links
        side = 0 if d < 0 else 1
        there = jnp.clip(k.z - d, 0, k.layers - 1)
        return k.remote(
            self.held(d, s - 1), self.relayed[d, s], self.z_send.at[side, s],
            self.z_recv.at[side, s], there * k.plane + k.q,
        )

    def spread(self, layer, e):
        k = self.links
        return k.remote(
            self.send.at[layer, e], self.near.at[layer * k.plane + k.q],
            self.p_send.at[layer, e], self.p_recv.at[layer, e], k.z * k.plane + k.qs[e],
        )

    def pack(self, d, s, e):
        k = self.links
        source, layer = self.held(d, s), self.layer(d, s)

        def put(spot, value):
            if e == 0:
                self.near[layer * k.plane + k.q, spot] = value
            else:
                self.send[layer, e, spot] = value

        if self.tail:
            row = lax.broadcasted_iota(jnp.int32, (TAIL, 128), 0)
            tile = jnp.zeros((TAIL, 128), f32)
            every = source[self.last].astype(f32)
        for c in range(self.capacity):
            index = jnp.maximum(self.table[(k.qs[e] * k.layers + layer) * self.capacity + c], 0)
            for i in range(self.tiles):
                put(c * self.tiles + i, source[index * self.tiles + i])
            if self.tail:
                line = jnp.sum(jnp.where(row == index, every, 0.0), axis=0, keepdims=True)
                tile = jnp.where(row == c, line, tile)
        if self.tail:
            put(self.capacity * self.tiles, tile.astype(bf16))

    def serve(self, d, s):
        for e in reversed(range(self.links.plane)):
            self.pack(d, s, e)
            if e:
                self.spread(self.layer(d, s), e).start()

    def start(self):
        for d in (-1, 1):
            @pl.when(inside(self.links.z - d, self.links.layers))
            def _():
                self.hop(d, 0).start()

    def advance(self, d, s):
        z, layers = self.links.z, self.links.layers

        @pl.when(inside(z + d * (s + 1), layers))
        def _():
            self.hop(d, s).wait_recv()
        if s < layers - 2:
            @pl.when(inside(z + d * (s + 1), layers) & inside(z - d, layers))
            def _():
                self.hop(d, s + 1).start()

        @pl.when(inside(z + d * (s + 1), layers))
        def _():
            self.serve(d, s)

    def finish(self):
        z, layers = self.links.z, self.links.layers
        for d in (-1, 1):
            for s in range(layers - 1):
                @pl.when(inside(z - d, layers) & inside(z + d * s, layers))
                def _():
                    self.hop(d, s).wait_send()
        for layer in range(layers):
            for e in range(1, self.links.plane):
                self.spread(layer, e).wait_recv()
                self.spread(layer, e).wait_send()


class Push:
    def __init__(self, links, slot_ref, lanes_ref, capacity, count, refs):
        self.links, self.slot, self.lanes, self.capacity, self.count = (
            links, slot_ref, lanes_ref, capacity, count,
        )
        self.given, self.out, self.arrive, self.zout, self.zin, *sems = refs
        self.z_send, self.z_recv, self.p_send, self.p_recv = sems
        self.group = self.out.shape[1]
        self.tiles = self.group // capacity

    def spread(self, o, e):
        k = self.links
        here = pl.ds(pl.multiple_of(k.q * self.group, self.group), self.group)
        return k.remote(
            self.out.at[k.zs[o] * k.plane + k.qs[e]], self.arrive.at[k.zs[o], here],
            self.p_send.at[o, e], self.p_recv.at[o, e], k.z * k.plane + k.qs[e],
        )

    def hop(self, o):
        k = self.links
        return k.remote(
            self.zout.at[o - 1], self.zin.at[o - 1], self.z_send.at[o - 1],
            self.z_recv.at[o - 1], k.zs[o] * k.plane + k.q,
        )

    def order(self):
        return list(reversed(range(1, self.links.layers)))

    def serve(self, o):
        k = self.links
        for e in reversed(range(k.plane)):
            device = k.zs[o] * k.plane + k.qs[e]
            for c in range(self.capacity):
                index = jnp.maximum(self.slot[device * self.capacity + c], 0)
                for i in range(self.tiles):
                    value = self.given[index * self.tiles + i]
                    if e:
                        self.out[device, c * self.tiles + i] = value
                    else:
                        self.arrive[k.zs[o], k.q * self.group + c * self.tiles + i] = value
            if e:
                self.spread(o, e).start()

    def gathered(self, o):
        k = self.links
        for e in range(1, k.plane):
            self.spread(o, e).wait_recv()
        arrived = self.arrive[k.zs[o]]
        arrived = arrived.reshape(-1, arrived.shape[-1])
        vec = self.tiles * arrived.shape[0] // (k.plane * self.group)
        lanes = self.lanes[pl.ds(k.zs[o], 1), :]
        shape = (vec, arrived.shape[0])
        row = lax.broadcasted_iota(jnp.int32, shape, 0)
        col = lax.broadcasted_iota(jnp.int32, shape, 1)
        same = row == lax.rem(col, vec)
        pick = [jnp.where(same & (lanes == i), 1.0, 0.0).astype(bf16) for i in range(self.count)]
        return dot_nn(jnp.concatenate(pick, axis=0), arrived)

    def advance(self, o):
        self.zout[o - 1] = self.gathered(o).astype(bf16)
        self.hop(o).start()

    def finish(self):
        total = self.gathered(0)
        for o in self.order():
            self.hop(o).wait_recv()
            total = total + self.zin[o - 1].astype(f32)
        for o in range(self.links.layers):
            if o:
                self.hop(o).wait_send()
            for e in range(1, self.links.plane):
                self.spread(o, e).wait_send()
        return total


def whole_kernel(
    geometry, factor, scale, counts,
    table_ref, slot_ref, target_ref, rank_ref, lanes_ref, noise_ref, shift_ref, c_ref, v_ref,
    result_ref, *scratch,
):
    total, layers, capacity = geometry
    count, size, _ = noise_ref.shape
    vec = v_ref.shape[0]
    half = size // 2
    scratch = list(scratch)
    take = lambda k: [scratch.pop(0) for _ in range(k)]
    d_ref, e_ref, u_ref, p_ref, rest_ref, m, pscr, qscr = take(8)
    pad = m.shape[0] // size
    links = Links(total, layers)
    pull_e = Pull(links, table_ref, capacity, count, 1, take(counts[0]))
    pull_left = Pull(links, table_ref, capacity, count, 0, take(counts[0]))
    pull_t = Pull(links, table_ref, capacity, count, 0, take(counts[0]))
    push_w = Push(links, slot_ref, lanes_ref, capacity, count, take(counts[1]))
    push_p = Push(links, slot_ref, lanes_ref, capacity, count, take(counts[1]))

    barrier = pltpu.get_barrier_semaphore()
    for device in links.partners():
        pl.semaphore_signal(barrier, inc=1, device_id=(device,), device_id_type=MESH)

    row_full = lax.broadcasted_iota(jnp.int32, (size, size), 0)
    col_full = lax.broadcasted_iota(jnp.int32, (size, size), 1)
    on_diag = row_full == col_full
    for n in range(count):
        noise = noise_ref[n].astype(f32)
        d = (noise + noise.T) * (0.5 * factor)
        d = d + jnp.where(on_diag, shift_ref[pl.ds(n, 1), :], 0.0)
        d_ref[n] = d
        m[pl.ds(n * size, size), :] = d
        if n < pad - count:
            m[pl.ds((count + n) * size, size), :] = d
    eliminate(m, pscr, qscr, count, pad, size)
    row = lax.broadcasted_iota(jnp.int32, (half, half), 0)
    col = lax.broadcasted_iota(jnp.int32, (half, half), 1)
    tail_row = lax.broadcasted_iota(jnp.int32, (TAIL, size), 0)
    tile = jnp.zeros((TAIL, size), f32)
    parts = half // TAIL
    for n in range(count):
        h, low = split2(m[pl.ds(n * size, size), :])
        e = tdot(jnp.concatenate([h, h, low], axis=0), jnp.concatenate([h, low, h], axis=0))
        e_ref[n] = e.astype(bf16)
        left = jnp.where(row >= col, e[:half, :half], e[half:, half:])
        packed = joined(left, e[:half, half:]).astype(bf16)
        for i in range(parts):
            pull_e.own[n * parts + i] = packed[i * TAIL : (i + 1) * TAIL]
        diag = jnp.sum(jnp.where(on_diag, e, 0.0), axis=0, keepdims=True)
        tile = jnp.where(tail_row == n, diag, tile)
    pull_e.own[count * parts] = tile.astype(bf16)

    pl.semaphore_wait(barrier, len(links.partners()))
    pull_e.start()
    pull_e.serve(0, -1)
    for s in range(layers - 1):
        pull_e.advance(-1, s)
        pull_e.advance(1, s)
    pull_e.finish()

    def schur(n, carry):
        fs, cs = [], []
        for k in range(3):
            t = target_ref[3 * n + k]
            c = rank_ref[3 * n + k]
            packed = jnp.concatenate(
                [pull_e.near[t, c * parts + i] for i in range(parts)], axis=0
            ).astype(f32)
            tile = pull_e.near[t, capacity * parts].astype(f32)
            diag = jnp.sum(jnp.where(tail_row == c, tile, 0.0), axis=0, keepdims=True)
            flipped = packed.T
            part = packed[:, :half]
            part_t = flipped[:half, :]
            first = jnp.where(row >= col, part, part_t)
            last = jnp.where(row < col, part, part_t)
            last = jnp.where(row == col, diag[:, half:], last)
            inverse = jnp.concatenate(
                [joined(first, packed[:, half:]), joined(flipped[half:, :], last)], axis=0
            ).astype(bf16)
            coupling = c_ref[n, k]
            fs.append((dot_nn(coupling, inverse) * (scale * scale)).astype(bf16))
            cs.append(coupling)
        reduced = d_ref[n] - dot_nt(joined(*fs), joined(*cs))
        m[pl.ds(pl.multiple_of(n * size, size), size), :] = reduced
        return carry

    lax.fori_loop(0, count, schur, 0, unroll=UNROLL)
    for n in range(count, pad):
        m[pl.ds(n * size, size), :] = d_ref[0]
    eliminate(m, pscr, qscr, count, pad, size)

    def give(push, n, x):
        low = (x * scale).astype(bf16)
        for k in range(3):
            value = dot_nn(low, c_ref[n, k]).astype(bf16)
            for i in range(vec // TAIL):
                push.given[(3 * n + k) * (vec // TAIL) + i] = value[i * TAIL : (i + 1) * TAIL]

    def offer(pull, n, x):
        for i in range(vec // TAIL):
            pull.own[n * (vec // TAIL) + i] = x[i * TAIL : (i + 1) * TAIL].astype(bf16)

    def pulled(pull, n):
        got, cs = [], []
        for k in range(3):
            t = target_ref[3 * n + k]
            c = rank_ref[3 * n + k]
            parts = vec // TAIL
            got.append(jnp.concatenate([pull.near[t, c * parts + i] for i in range(parts)], axis=0))
            cs.append(c_ref[n, k])
        return scale * dot_nt(joined(*got), joined(*cs))

    for n in range(count):
        kh, kl = split2(m[pl.ds(n * size, size), :])
        vh, vl = split2(v_ref[:, n * size : (n + 1) * size])
        u = dot_nn(joined(vh, vh, vl), jnp.concatenate([kh, kl, kh], axis=0))
        u_ref[n] = u
        give(push_w, n, u)
    for o in push_w.order() + [0]:
        push_w.serve(o)
    for n in range(count):
        uh, ul = split2(u_ref[n])
        dh, dl = split2(d_ref[n])
        rest_ref[n] = dot_nn(joined(uh, uh, ul), jnp.concatenate([dh, dl, dh], axis=0))
    for o in push_w.order():
        push_w.advance(o)
    w = push_w.finish().astype(bf16)

    for n in range(count):
        p = dot_nn(w[n * vec : (n + 1) * vec], e_ref[n])
        p_ref[n] = p
        offer(pull_left, n, u_ref[n] - p)
        give(push_p, n, p)
    pull_left.start()
    for o in push_p.order() + [0]:
        push_p.serve(o)
    pull_left.serve(0, -1)
    for s, o in enumerate(push_p.order()):
        push_p.advance(o)
        pull_left.advance(-1, s)
        pull_left.advance(1, s)
    pushed = push_p.finish()
    pull_left.finish()

    for n in range(count):
        sent = pushed[n * vec : (n + 1) * vec]
        q = pulled(pull_left, n) - sent
        t = p_ref[n] + dot_nn(q.astype(bf16), e_ref[n])
        offer(pull_t, n, t)
        rest_ref[n] = rest_ref[n] - sent
    pull_t.start()
    pull_t.serve(0, -1)
    for s in range(layers - 1):
        pull_t.advance(-1, s)
        pull_t.advance(1, s)
    pull_t.finish()

    for n in range(count):
        part = rest_ref[n] - pulled(pull_t, n)
        ph, plow = split2(part)
        kh, kl = split2(m[pl.ds(n * size, size), :])
        result_ref[:, n * size : (n + 1) * size] = dot_nt(
            joined(ph, ph, plow), joined(kh, kl, kh)
        )


def run(geometry, factor, scale, scalars, arrays, row_count, block_size, vec_count):
    total, layers, capacity = geometry
    plane = total // layers
    smem = pl.BlockSpec(memory_space=pltpu.SMEM)
    vmem = pl.BlockSpec(memory_space=pltpu.VMEM)
    dma = pltpu.SemaphoreType.DMA
    pad = -(-row_count // 8) * 8
    block_shape = (row_count, block_size, block_size)
    rows_shape = (row_count, vec_count, block_size)
    scratch = [
        pltpu.VMEM(block_shape, f32),
        pltpu.VMEM(block_shape, bf16),
        pltpu.VMEM(rows_shape, f32),
        pltpu.VMEM(rows_shape, f32),
        pltpu.VMEM(rows_shape, f32),
        pltpu.VMEM((pad * block_size, block_size), f32),
        pltpu.VMEM((PANEL * pad, block_size), f32),
        pltpu.VMEM((PANEL * pad, block_size), f32),
    ]
    vec_tiles = vec_count // TAIL
    pull_count = push_count = 0

    def tiles(*shape):
        return pltpu.VMEM(shape + (TAIL, block_size), bf16)

    for parts, tail in ((block_size // 2 // TAIL, 1), (vec_tiles, 0), (vec_tiles, 0)):
        own, group = row_count * parts + tail, capacity * parts + tail
        pulls = [tiles(own), tiles(layers, plane, group), tiles(total, group)]
        pulls += [tiles(own)] * (2 * layers - 2)
        pulls += [dma((2, layers - 1))] * 2 + [dma((layers, plane))] * 2
        pull_count = len(pulls)
        scratch += pulls
    for _ in range(2):
        group = capacity * vec_tiles
        pushes = [tiles(row_count * 3 * vec_tiles), tiles(total, group), tiles(layers, plane * group)]
        pushes += [pltpu.VMEM((layers - 1, row_count * vec_count, block_size), bf16)] * 2
        pushes += [dma((layers - 1,))] * 2 + [dma((layers, plane))] * 2
        push_count = len(pushes)
        scratch += pushes
    return pl.pallas_call(
        functools.partial(whole_kernel, geometry, factor, scale, (pull_count, push_count)),
        out_shape=jax.ShapeDtypeStruct((vec_count, row_count * block_size), f32),
        in_specs=[smem] * len(scalars) + [vmem] * len(arrays),
        out_specs=vmem,
        scratch_shapes=scratch,
        compiler_params=pltpu.CompilerParams(collective_id=0, has_side_effects=True),
    )(*scalars, *arrays)


def body(diag_noise, couplings, shifts, near_devices, near_slots, vectors):
    dev_count = lax.axis_size("rows")
    my_index = lax.axis_index("rows")
    row_count, block_size = diag_noise.shape[:2]
    vec_count = vectors.shape[0]
    capacity = 3 * row_count // (dev_count - 1) + 2
    layers = LAYERS
    plane = dev_count // layers
    factor = 0.5 / math.sqrt(block_size)
    scale = 0.4 / math.sqrt(block_size)

    target = ((my_index - 1 - near_devices) % dev_count).reshape(-1)
    device_onehot = (target[:, None] == jnp.arange(dev_count, dtype=jnp.int32)[None, :]).astype(
        jnp.int32
    )
    running = jnp.cumsum(device_onehot, axis=0) - 1
    rank = jnp.sum(running * device_onehot, axis=1)
    position = (target % plane * layers + target // plane) * capacity + rank
    every = jnp.arange(dev_count * capacity, dtype=jnp.int32)[:, None]
    hit = position[None, :] == every
    asked = jnp.sum(jnp.where(hit, near_slots.reshape(1, -1) + 1, 0), axis=1) - 1
    hit = (target * capacity + rank)[None, :] == every
    slot = jnp.sum(jnp.where(hit, jnp.arange(3 * row_count, dtype=jnp.int32)[None, :], 0), axis=1)
    groups = [[i * plane + j for j in range(plane)] for i in range(layers)]
    table = lax.all_to_all(
        asked.reshape(plane, layers * capacity), "rows", 0, 0,
        axis_index_groups=groups, tiled=True,
    ).reshape(-1)
    lanes = table.reshape(plane, layers, capacity).transpose(1, 0, 2)
    lanes = jnp.repeat(lanes.reshape(layers, -1), vec_count, axis=1)
    return run(
        (dev_count, layers, capacity), factor, scale,
        (table, slot, target, rank),
        (lanes, diag_noise, shifts.astype(f32), couplings, vectors),
        row_count, block_size, vec_count,
    )


def solution(mesh):
    return jax.shard_map(
        body,
        mesh=mesh,
        in_specs=(
            P("rows", None, None),
            P("rows", None, None, None),
            P("rows", None),
            P("rows", None),
            P("rows", None),
            P(None, "rows"),
        ),
        out_specs=P(None, "rows"),
        check_vma=False,
    )
```

```python
import functools
import math

import jax
import jax.numpy as jnp
from jax import lax
from jax.experimental import pallas as pl
from jax.experimental.pallas import tpu as pltpu
from jax.sharding import PartitionSpec as P

PANEL = 16
GROUP = 4
LAYERS = 4
TAIL = 16
UNROLL = 7
MESH = pl.DeviceIdType.MESH
bf16, f32 = jnp.bfloat16, jnp.float32


def split2(x):
    high = x.astype(bf16)
    return high, (x - high.astype(f32)).astype(bf16)


def joined(*parts):
    return jnp.concatenate(parts, axis=-1)


def tdot(a, b):
    return lax.dot_general(a, b, (((0,), (0,)), ((), ())), preferred_element_type=f32)


def dot_nn(a, b):
    return jnp.dot(a, b, preferred_element_type=f32)


def dot_nt(a, b):
    return lax.dot_general(a, b, (((1,), (1,)), ((), ())), preferred_element_type=f32)


def eliminate(m, pscr, qscr, count, pad, size, hook=None):
    panel = PANEL
    lane = lax.broadcasted_iota(jnp.int32, (pad, size), 1)
    for block in reversed(range(size // panel)):
        base = block * panel
        rows = [m[pl.ds(base + r, pad, stride=size), :] for r in range(panel)]
        for k in reversed(range(panel)):
            col = base + k
            here = lane == col
            if (k + 1) % GROUP == 0:
                first = k + 1 - GROUP
                tile = {
                    (i, c): jnp.broadcast_to(rows[i][:, base + c : base + c + 1], (pad, size))
                    for c in range(first, k + 1)
                    for i in range(c + 1)
                }
            inv = 1.0 / tile[k, k]
            for c in reversed(range(first, k)):
                ratio = tile[c, k] * inv
                for i in range(c + 1):
                    tile[i, c] = tile[i, c] - tile[i, k] * ratio
            pivot_row = jnp.where(here, 1.0, rows[k])
            scaled = pivot_row * inv
            step = jnp.where(here, 1.0 + inv, scaled)
            for i in range(k):
                rows[i] = rows[i] - tile[i, k] * step
            if block:
                pscr[pl.ds(k * pad, pad), :] = jnp.where(
                    (lane >= base) & (lane < col), 0.0, pivot_row
                )
                qscr[pl.ds(k * pad, pad), :] = scaled
            m[pl.ds(col, pad, stride=size), :] = jnp.where(
                lane >= col, pivot_row * jnp.sqrt(inv), 0.0
            )
        if block:
            lane_m = lax.broadcasted_iota(jnp.int32, (base, size), 1)
            inside = (lane_m >= base) & (lane_m < base + panel)
            for n in range(count):
                ph, plow = split2(pscr[pl.ds(n, panel, stride=pad), :])
                qh, qlow = split2(qscr[pl.ds(n, panel, stride=pad), :])
                right = jnp.concatenate([ph, plow, ph], axis=0)
                left = jnp.concatenate([qh, qh, qlow], axis=0)
                update = tdot(left, right)[:base]
                spot = pl.ds(n * size, base)
                m[spot, :] = jnp.where(inside, 0.0, m[spot, :]) - update
        if hook and block * 2 == size // panel:
            hook()


def inside(x, layers):
    return (x >= 0) & (x < layers)


class Links:
    def __init__(self, total, layers):
        self.layers, self.plane = layers, total // layers
        me = lax.axis_index("rows")
        self.z = me // self.plane
        self.q = lax.rem(me, self.plane)
        self.zs = [jnp.bitwise_xor(self.z, o) for o in range(layers)]
        self.qs = [jnp.bitwise_xor(self.q, e) for e in range(self.plane)]

    def partners(self):
        far = [self.zs[o] * self.plane + self.q for o in range(1, self.layers)]
        return far + [self.z * self.plane + self.qs[e] for e in range(1, self.plane)]

    def remote(self, src, dst, send, recv, device):
        return pltpu.make_async_remote_copy(
            src_ref=src, dst_ref=dst, send_sem=send, recv_sem=recv,
            device_id=(device,), device_id_type=MESH,
        )


class Pull:
    def __init__(self, links, table_ref, capacity, count, tail, refs):
        self.links, self.table, self.capacity, self.tail = links, table_ref, capacity, tail
        self.own, self.send, self.near, *rest = refs
        moves = [(d, s) for s in range(links.layers - 1) for d in (-1, 1)]
        self.relayed = dict(zip(moves, rest))
        self.z_send, self.z_recv, self.p_send, self.p_recv = rest[len(moves):]
        self.tiles = (self.own.shape[0] - tail) // count
        self.last = count * self.tiles
        self.group = capacity * self.tiles + tail

    def held(self, d, s):
        return self.own if s < 0 else self.relayed[d, s]

    def layer(self, d, s):
        return self.links.z if s < 0 else jnp.clip(self.links.z + d * (s + 1), 0, self.links.layers - 1)

    def hop(self, d, s):
        k = self.links
        side = 0 if d < 0 else 1
        there = jnp.clip(k.z - d, 0, k.layers - 1)
        return k.remote(
            self.held(d, s - 1), self.relayed[d, s], self.z_send.at[side, s],
            self.z_recv.at[side, s], there * k.plane + k.q,
        )

    def spread(self, layer, e):
        k = self.links
        return k.remote(
            self.send.at[layer, e], self.near.at[layer * k.plane + k.q],
            self.p_send.at[layer, e], self.p_recv.at[layer, e], k.z * k.plane + k.qs[e],
        )

    def pack(self, d, s, e):
        k = self.links
        source, layer = self.held(d, s), self.layer(d, s)

        def put(spot, value):
            if e == 0:
                self.near[layer * k.plane + k.q, spot] = value
            else:
                self.send[layer, e, spot] = value

        if self.tail:
            row = lax.broadcasted_iota(jnp.int32, (TAIL, 128), 0)
            tile = jnp.zeros((TAIL, 128), f32)
            every = source[self.last].astype(f32)
        for c in range(self.capacity):
            index = jnp.maximum(self.table[k.qs[e], 0, layer * self.capacity + c], 0)
            for i in range(self.tiles):
                put(c * self.tiles + i, source[index * self.tiles + i])
            if self.tail:
                line = jnp.sum(jnp.where(row == index, every, 0.0), axis=0, keepdims=True)
                tile = jnp.where(row == c, line, tile)
        if self.tail:
            put(self.capacity * self.tiles, tile.astype(bf16))

    def serve(self, d, s):
        for e in reversed(range(self.links.plane)):
            self.pack(d, s, e)
            if e:
                self.spread(self.layer(d, s), e).start()

    def start(self):
        for d in (-1, 1):
            @pl.when(inside(self.links.z - d, self.links.layers))
            def _():
                self.hop(d, 0).start()

    def advance(self, d, s):
        z, layers = self.links.z, self.links.layers

        @pl.when(inside(z + d * (s + 1), layers))
        def _():
            self.hop(d, s).wait_recv()
        if s < layers - 2:
            @pl.when(inside(z + d * (s + 1), layers) & inside(z - d, layers))
            def _():
                self.hop(d, s + 1).start()

        @pl.when(inside(z + d * (s + 1), layers))
        def _():
            self.serve(d, s)

    def finish(self):
        for layer in range(self.links.layers):
            for e in range(1, self.links.plane):
                self.spread(layer, e).wait_recv()

    def drain(self):
        z, layers = self.links.z, self.links.layers
        for d in (-1, 1):
            for s in range(layers - 1):
                @pl.when(inside(z - d, layers) & inside(z + d * s, layers))
                def _():
                    self.hop(d, s).wait_send()
        for layer in range(layers):
            for e in range(1, self.links.plane):
                self.spread(layer, e).wait_send()


class Push:
    def __init__(self, links, slot_ref, lanes_ref, capacity, count, refs):
        self.links, self.slot, self.lanes, self.capacity, self.count = (
            links, slot_ref, lanes_ref, capacity, count,
        )
        self.given, self.out, self.arrive, self.zout, self.zin, *sems = refs
        self.z_send, self.z_recv, self.p_send, self.p_recv = sems
        self.group = self.out.shape[1]
        self.tiles = self.group // capacity

    def spread(self, o, e):
        k = self.links
        here = pl.ds(pl.multiple_of(k.q * self.group, self.group), self.group)
        return k.remote(
            self.out.at[k.zs[o] * k.plane + k.qs[e]], self.arrive.at[k.zs[o], here],
            self.p_send.at[o, e], self.p_recv.at[o, e], k.z * k.plane + k.qs[e],
        )

    def hop(self, o):
        k = self.links
        return k.remote(
            self.zout.at[o - 1], self.zin.at[o - 1], self.z_send.at[o - 1],
            self.z_recv.at[o - 1], k.zs[o] * k.plane + k.q,
        )

    def order(self):
        return list(reversed(range(1, self.links.layers)))

    def serve(self, o):
        k = self.links
        for e in reversed(range(k.plane)):
            device = k.zs[o] * k.plane + k.qs[e]
            for c in range(self.capacity):
                index = jnp.maximum(self.slot[device * self.capacity + c], 0)
                for i in range(self.tiles):
                    value = self.given[index * self.tiles + i]
                    if e:
                        self.out[device, c * self.tiles + i] = value
                    else:
                        self.arrive[k.zs[o], k.q * self.group + c * self.tiles + i] = value
            if e:
                self.spread(o, e).start()

    def gathered(self, o):
        k = self.links
        for e in range(1, k.plane):
            self.spread(o, e).wait_recv()
        arrived = self.arrive[k.zs[o]]
        arrived = arrived.reshape(-1, arrived.shape[-1])
        vec = self.tiles * arrived.shape[0] // (k.plane * self.group)
        lanes = self.lanes[k.zs[o]][:1]
        shape = (vec, arrived.shape[0])
        row = lax.broadcasted_iota(jnp.int32, shape, 0)
        col = lax.broadcasted_iota(jnp.int32, shape, 1)
        same = row == lax.rem(col, vec)
        pick = [jnp.where(same & (lanes == i), 1.0, 0.0).astype(bf16) for i in range(self.count)]
        return dot_nn(jnp.concatenate(pick, axis=0), arrived)

    def advance(self, o):
        self.zout[o - 1] = self.gathered(o).astype(bf16)
        self.hop(o).start()

    def finish(self):
        total = self.gathered(0)
        for o in self.order():
            self.hop(o).wait_recv()
            total = total + self.zin[o - 1].astype(f32)
        return total

    def drain(self):
        for o in range(self.links.layers):
            if o:
                self.hop(o).wait_send()
            for e in range(1, self.links.plane):
                self.spread(o, e).wait_send()


def index_kernel(
    total, layers, capacity, near_ref, target_ref, rank_ref, slot_ref, asked_ref, seen_ref
):
    plane = total // layers
    me = lax.axis_index("rows")
    width = 3
    count = near_ref.shape[0] // width

    def clear(i, carry):
        seen_ref[i] = 0
        for c in range(capacity):
            slot_ref[i * capacity + c] = 0
            asked_ref[i * capacity + c] = -1
        return carry

    def place(n, carry):
        for k in range(width):
            r = n * width + k
            wanted = near_ref[r]
            t = me - 1 - wanted // count
            t = jnp.where(t < 0, t + total, t)
            c = seen_ref[t]
            seen_ref[t] = c + 1
            target_ref[r] = t
            rank_ref[r] = c
            slot_ref[t * capacity + c] = r
            asked_ref[(lax.rem(t, plane) * layers + t // plane) * capacity + c] = lax.rem(wanted, count)
        return carry

    lax.fori_loop(0, total, clear, 0)
    lax.fori_loop(0, count, place, 0)


def whole_kernel(
    geometry, factor, scale, counts,
    target_ref, rank_ref, slot_ref, asked_ref, noise_ref, shift_ref, c_ref, v_ref,
    result_ref, *scratch,
):
    total, layers, capacity = geometry
    count, size, _ = noise_ref.shape
    vec = v_ref.shape[0]
    half = size // 2
    scratch = list(scratch)
    take = lambda k: [scratch.pop(0) for _ in range(k)]
    d_ref, e_ref, u_ref, p_ref, rest_ref, m, pscr, qscr = take(8)
    pad = m.shape[0] // size
    links = Links(total, layers)
    lanes_ref, ask_out, ask_in, table_ref, ask_send, ask_recv, table_sem = take(7)
    shares = vec // TAIL
    split = range(shares)

    def pulls(tails):
        return [Pull(links, table_ref, capacity, count, tail, take(counts[0])) for tail in tails]

    def pushes():
        return [Push(links, slot_ref, lanes_ref, capacity, count, take(counts[1])) for _ in split]

    pull_e, pull_left, pull_t = pulls((0, 1)), pulls((0,) * shares), pulls((0,) * shares)
    push_w, push_p = pushes(), pushes()

    barrier = pltpu.get_barrier_semaphore()
    for device in links.partners():
        pl.semaphore_signal(barrier, inc=1, device_id=(device,), device_id_type=MESH)

    row_full = lax.broadcasted_iota(jnp.int32, (size, size), 0)
    col_full = lax.broadcasted_iota(jnp.int32, (size, size), 1)
    on_diag = row_full == col_full
    shifts = shift_ref[...].astype(f32)
    for n in range(count):
        noise = noise_ref[n].astype(f32)
        d = (noise + noise.T) * (0.5 * factor)
        d = d + jnp.where(on_diag, shifts[n : n + 1], 0.0)
        d_ref[n] = d
        m[pl.ds(n * size, size), :] = d
        if n < pad - count:
            m[pl.ds((count + n) * size, size), :] = d

    plane = links.plane
    asks = layers * capacity
    ask_lane = lax.broadcasted_iota(jnp.int32, ask_out.shape[1:], 1)

    def ask(e):
        return links.remote(
            ask_out.at[links.qs[e]], ask_in.at[links.q], ask_send.at[e], ask_recv.at[e],
            links.z * plane + links.qs[e],
        )

    def exchange_asks():
        for other in range(plane):
            line = jnp.zeros(ask_out.shape[1:], jnp.int32)
            for i in range(asks):
                line = jnp.where(ask_lane == i, asked_ref[other * asks + i], line)
            ask_out[other] = line
        pl.semaphore_wait(barrier, len(links.partners()))
        ask_in[links.q] = ask_out[links.q]
        for e in range(1, plane):
            ask(e).start()

    eliminate(m, pscr, qscr, count, pad, size, exchange_asks)
    for e in range(1, plane):
        ask(e).wait()
    table_copy = pltpu.make_async_copy(ask_in, table_ref, table_sem)
    table_copy.start()
    row = lax.broadcasted_iota(jnp.int32, (half, half), 0)
    col = lax.broadcasted_iota(jnp.int32, (half, half), 1)
    tail_row = lax.broadcasted_iota(jnp.int32, (TAIL, size), 0)
    tile = jnp.zeros((TAIL, size), f32)
    parts = half // TAIL // 2
    for n in range(count):
        h, low = split2(m[pl.ds(n * size, size), :])
        e = tdot(jnp.concatenate([h, h, low], axis=0), jnp.concatenate([h, low, h], axis=0))
        e_ref[n] = e.astype(bf16)
        left = jnp.where(row >= col, e[:half, :half], e[half:, half:])
        packed = joined(left, e[:half, half:]).astype(bf16)
        for i in range(parts):
            for j in range(2):
                first = (j * parts + i) * TAIL
                pull_e[j].own[n * parts + i] = packed[first : first + TAIL]
        diag = jnp.sum(jnp.where(on_diag, e, 0.0), axis=0, keepdims=True)
        tile = jnp.where(tail_row == n, diag, tile)
    pull_e[1].own[count * parts] = tile.astype(bf16)

    for pull in pull_e:
        pull.start()
    table_copy.wait()
    for pull in pull_e:
        pull.serve(0, -1)
    width = size // TAIL
    lane = lax.broadcasted_iota(jnp.int32, (8, size), 1) // TAIL
    for layer in range(layers):
        for i in range(plane * capacity // width):
            line = jnp.zeros((8, size), jnp.int32)
            for j in range(width):
                other, c = divmod(i * width + j, capacity)
                line = jnp.where(lane == j, table_ref[other, 0, layer * capacity + c], line)
            lanes_ref[layer, :, i * size : (i + 1) * size] = line
    for s in range(layers - 1):
        for pull in pull_e:
            pull.advance(-1, s)
            pull.advance(1, s)
    for pull in pull_e:
        pull.finish()

    def schur(n, carry):
        fs, cs = [], []
        for k in range(3):
            t = target_ref[3 * n + k]
            c = rank_ref[3 * n + k]
            packed = jnp.concatenate(
                [pull.near[t, c * parts + i] for pull in pull_e for i in range(parts)], axis=0
            ).astype(f32)
            tile = pull_e[1].near[t, capacity * parts].astype(f32)
            diag = jnp.sum(jnp.where(tail_row == c, tile, 0.0), axis=0, keepdims=True)
            flipped = packed.T
            part = packed[:, :half]
            part_t = flipped[:half, :]
            first = jnp.where(row >= col, part, part_t)
            last = jnp.where(row < col, part, part_t)
            last = jnp.where(row == col, diag[:, half:], last)
            inverse = jnp.concatenate(
                [joined(first, packed[:, half:]), joined(flipped[half:, :], last)], axis=0
            ).astype(bf16)
            coupling = c_ref[n, k]
            fs.append((dot_nn(coupling, inverse) * (scale * scale)).astype(bf16))
            cs.append(coupling)
        reduced = d_ref[n] - dot_nt(joined(*fs), joined(*cs))
        m[pl.ds(pl.multiple_of(n * size, size), size), :] = reduced
        return carry

    lax.fori_loop(0, count, schur, 0, unroll=UNROLL)
    for n in range(count, pad):
        m[pl.ds(n * size, size), :] = d_ref[0]
    eliminate(m, pscr, qscr, count, pad, size)

    def give(push, n, x):
        low = (x * scale).astype(bf16)
        for k in range(3):
            value = dot_nn(low, c_ref[n, k]).astype(bf16)
            for i, part in enumerate(push):
                part.given[3 * n + k] = value[i * TAIL : (i + 1) * TAIL]

    def pulled(pull, n):
        got = [pull.near[target_ref[3 * n + k], rank_ref[3 * n + k]] for k in range(3)]
        return scale * dot_nt(joined(*got), joined(*[c_ref[n, k] for k in range(3)]))

    for n in range(count):
        kh, kl = split2(m[pl.ds(n * size, size), :])
        vh, vl = split2(v_ref[:, n * size : (n + 1) * size])
        u = dot_nn(joined(vh, vh, vl), jnp.concatenate([kh, kl, kh], axis=0))
        u_ref[n] = u
        give(push_w, n, u)
    for push in push_w:
        for o in push.order() + [0]:
            push.serve(o)
    for n in range(count):
        uh, ul = split2(u_ref[n])
        dh, dl = split2(d_ref[n])
        rest_ref[n] = dot_nn(joined(uh, uh, ul), jnp.concatenate([dh, dl, dh], axis=0))
    for push in push_w:
        for o in push.order():
            push.advance(o)

    span = [slice(i * TAIL, (i + 1) * TAIL) for i in split]
    for i in split:
        w = push_w[i].finish().astype(bf16)
        for n in range(count):
            p = dot_nn(w[n * TAIL : (n + 1) * TAIL], e_ref[n])
            p_ref[n, span[i], :] = p
            pull_left[i].own[n] = (u_ref[n, span[i], :] - p).astype(bf16)
            give(push_p[i : i + 1], n, p)
        pull_left[i].start()
        for o in push_p[i].order() + [0]:
            push_p[i].serve(o)
        pull_left[i].serve(0, -1)
    for i in split:
        for s, o in enumerate(push_p[i].order()):
            push_p[i].advance(o)
            pull_left[i].advance(-1, s)
            pull_left[i].advance(1, s)
    for i in split:
        pushed = push_p[i].finish()
        pull_left[i].finish()
        for n in range(count):
            sent = pushed[n * TAIL : (n + 1) * TAIL]
            q = pulled(pull_left[i], n) - sent
            t = p_ref[n, span[i], :] + dot_nn(q.astype(bf16), e_ref[n])
            pull_t[i].own[n] = t.astype(bf16)
            rest_ref[n, span[i], :] = rest_ref[n, span[i], :] - sent
        pull_t[i].start()
        pull_t[i].serve(0, -1)
    for i in split:
        for s in range(layers - 1):
            pull_t[i].advance(-1, s)
            pull_t[i].advance(1, s)
    for i in split:
        pull_t[i].finish()
        for n in range(count):
            part = rest_ref[n, span[i], :] - pulled(pull_t[i], n)
            ph, plow = split2(part)
            kh, kl = split2(m[pl.ds(n * size, size), :])
            result_ref[span[i], n * size : (n + 1) * size] = dot_nt(
                joined(ph, ph, plow), joined(kh, kl, kh)
            )
    for moved in pull_e + push_w + push_p + pull_left + pull_t:
        moved.drain()


def run(geometry, factor, scale, scalars, arrays, row_count, block_size, vec_count):
    total, layers, capacity = geometry
    plane = total // layers
    smem = pl.BlockSpec(memory_space=pltpu.SMEM)
    vmem = pl.BlockSpec(memory_space=pltpu.VMEM)
    dma = pltpu.SemaphoreType.DMA
    pad = -(-row_count // 8) * 8
    block_shape = (row_count, block_size, block_size)
    rows_shape = (row_count, vec_count, block_size)
    scratch = [
        pltpu.VMEM(block_shape, f32),
        pltpu.VMEM(block_shape, bf16),
        pltpu.VMEM(rows_shape, f32),
        pltpu.VMEM(rows_shape, f32),
        pltpu.VMEM(rows_shape, f32),
        pltpu.VMEM((pad * block_size, block_size), f32),
        pltpu.VMEM((PANEL * pad, block_size), f32),
        pltpu.VMEM((PANEL * pad, block_size), f32),
    ]
    scratch += [
        pltpu.VMEM((layers, 8, plane * capacity * TAIL), jnp.int32),
        pltpu.VMEM((plane, 8, block_size), jnp.int32),
        pltpu.VMEM((plane, 8, block_size), jnp.int32),
        pltpu.SMEM((plane, 8, block_size), jnp.int32),
        dma((plane,)),
        dma((plane,)),
        dma,
    ]
    shares = vec_count // TAIL
    pull_count = push_count = 0

    def tiles(*shape):
        return pltpu.VMEM(shape + (TAIL, block_size), bf16)

    quarter = block_size // 4 // TAIL
    for parts, tail in ((quarter, 0), (quarter, 1)) + ((1, 0),) * (2 * shares):
        own, group = row_count * parts + tail, capacity * parts + tail
        pulls = [tiles(own), tiles(layers, plane, group), tiles(total, group)]
        pulls += [tiles(own)] * (2 * layers - 2)
        pulls += [dma((2, layers - 1))] * 2 + [dma((layers, plane))] * 2
        pull_count = len(pulls)
        scratch += pulls
    for _ in range(2 * shares):
        pushes = [tiles(row_count * 3), tiles(total, capacity), tiles(layers, plane * capacity)]
        pushes += [pltpu.VMEM((layers - 1, row_count * TAIL, block_size), bf16)] * 2
        pushes += [dma((layers - 1,))] * 2 + [dma((layers, plane))] * 2
        push_count = len(pushes)
        scratch += pushes
    return pl.pallas_call(
        functools.partial(whole_kernel, geometry, factor, scale, (pull_count, push_count)),
        out_shape=jax.ShapeDtypeStruct((vec_count, row_count * block_size), f32),
        in_specs=[smem] * len(scalars) + [vmem] * len(arrays),
        out_specs=vmem,
        scratch_shapes=scratch,
        compiler_params=pltpu.CompilerParams(collective_id=0, has_side_effects=True),
    )(*scalars, *arrays)


def body(diag_noise, couplings, shifts, near_devices, near_slots, vectors):
    dev_count = lax.axis_size("rows")
    row_count, block_size = diag_noise.shape[:2]
    vec_count = vectors.shape[0]
    capacity = 3 * row_count // (dev_count - 1) + 2
    layers = LAYERS
    factor = 0.5 / math.sqrt(block_size)
    scale = 0.4 / math.sqrt(block_size)

    smem = pl.BlockSpec(memory_space=pltpu.SMEM)
    requests = 3 * row_count
    lengths = (requests, requests, dev_count * capacity, dev_count * capacity)
    tables = pl.pallas_call(
        functools.partial(index_kernel, dev_count, layers, capacity),
        out_shape=[jax.ShapeDtypeStruct((length,), jnp.int32) for length in lengths],
        in_specs=[smem],
        out_specs=[smem] * 4,
        scratch_shapes=[pltpu.SMEM((dev_count,), jnp.int32)],
    )((near_devices * row_count + near_slots).reshape(-1))
    return run(
        (dev_count, layers, capacity), factor, scale,
        tables,
        (diag_noise, shifts, couplings, vectors),
        row_count, block_size, vec_count,
    )


def solution(mesh):
    return jax.shard_map(
        body,
        mesh=mesh,
        in_specs=(
            P("rows", None, None),
            P("rows", None, None, None),
            P("rows", None),
            P("rows", None),
            P("rows", None),
            P(None, "rows"),
        ),
        out_specs=P(None, "rows"),
        check_vma=False,
    )
```

```python
import functools
import math

import jax
import jax.numpy as jnp
from jax import lax
from jax.experimental import pallas as pl
from jax.experimental.pallas import tpu as pltpu
from jax.sharding import PartitionSpec as P

PANEL = 16
GROUP = 4
LAYERS = 4
TAIL = 16
UNROLL = 7
STRIDE = 16
MESH = pl.DeviceIdType.MESH
bf16, f32 = jnp.bfloat16, jnp.float32


def split2(x):
    high = x.astype(bf16)
    return high, (x - high.astype(f32)).astype(bf16)


def joined(*parts):
    return jnp.concatenate(parts, axis=-1)


def tdot(a, b):
    return lax.dot_general(a, b, (((0,), (0,)), ((), ())), preferred_element_type=f32)


def dot_nn(a, b):
    return jnp.dot(a, b, preferred_element_type=f32)


def dot_nt(a, b):
    return lax.dot_general(a, b, (((1,), (1,)), ((), ())), preferred_element_type=f32)


def eliminate(m, pscr, qscr, count, pad, size, hook=None):
    panel = PANEL
    lane = lax.broadcasted_iota(jnp.int32, (pad, size), 1)
    for block in reversed(range(size // panel)):
        base = block * panel
        rows = [m[pl.ds(base + r, pad, stride=size), :] for r in range(panel)]
        for k in reversed(range(panel)):
            col = base + k
            here = lane == col
            if (k + 1) % GROUP == 0:
                first = k + 1 - GROUP
                tile = {
                    (i, c): jnp.broadcast_to(rows[i][:, base + c : base + c + 1], (pad, size))
                    for c in range(first, k + 1)
                    for i in range(c + 1)
                }
            inv = 1.0 / tile[k, k]
            for c in reversed(range(first, k)):
                ratio = tile[c, k] * inv
                for i in range(c + 1):
                    tile[i, c] = tile[i, c] - tile[i, k] * ratio
            pivot_row = jnp.where(here, 1.0, rows[k])
            scaled = pivot_row * inv
            step = jnp.where(here, 1.0 + inv, scaled)
            for i in range(k):
                rows[i] = rows[i] - tile[i, k] * step
            if block:
                pscr[pl.ds(k * pad, pad), :] = jnp.where(
                    (lane >= base) & (lane < col), 0.0, pivot_row
                )
                qscr[pl.ds(k * pad, pad), :] = scaled
            m[pl.ds(col, pad, stride=size), :] = jnp.where(
                lane >= col, pivot_row * jnp.sqrt(inv), 0.0
            )
        if block:
            lane_m = lax.broadcasted_iota(jnp.int32, (base, size), 1)
            inside = (lane_m >= base) & (lane_m < base + panel)
            for n in range(count):
                ph, plow = split2(pscr[pl.ds(n, panel, stride=pad), :])
                qh, qlow = split2(qscr[pl.ds(n, panel, stride=pad), :])
                right = jnp.concatenate([ph, plow, ph], axis=0)
                left = jnp.concatenate([qh, qh, qlow], axis=0)
                update = tdot(left[:, :base], right)
                spot = pl.ds(n * size, base)
                m[spot, :] = jnp.where(inside, 0.0, m[spot, :]) - update
        if hook and block * 2 == size // panel:
            hook()


def inside(x, layers):
    return (x >= 0) & (x < layers)


class Links:
    def __init__(self, total, layers):
        self.layers, self.plane = layers, total // layers
        me = lax.axis_index("rows")
        self.z = me // self.plane
        self.q = lax.rem(me, self.plane)
        self.zs = [jnp.bitwise_xor(self.z, o) for o in range(layers)]
        self.qs = [jnp.bitwise_xor(self.q, e) for e in range(self.plane)]

    def partners(self):
        far = [self.zs[o] * self.plane + self.q for o in range(1, self.layers)]
        return far + [self.z * self.plane + self.qs[e] for e in range(1, self.plane)]

    def remote(self, src, dst, send, recv, device):
        return pltpu.make_async_remote_copy(
            src_ref=src, dst_ref=dst, send_sem=send, recv_sem=recv,
            device_id=(device,), device_id_type=MESH,
        )


class Pull:
    def __init__(self, links, table_ref, capacity, count, tail, refs):
        self.links, self.table, self.capacity, self.tail = links, table_ref, capacity, tail
        self.own, self.send, self.near, *rest = refs
        moves = [(d, s) for s in range(links.layers - 1) for d in (-1, 1)]
        self.relayed = dict(zip(moves, rest))
        self.z_send, self.z_recv, self.p_send, self.p_recv = rest[len(moves):]
        self.tiles = (self.own.shape[0] - tail) // count
        self.last = count * self.tiles
        self.group = capacity * self.tiles + tail

    def held(self, d, s):
        return self.own if s < 0 else self.relayed[d, s]

    def layer(self, d, s):
        return self.links.z if s < 0 else jnp.clip(self.links.z + d * (s + 1), 0, self.links.layers - 1)

    def hop(self, d, s):
        k = self.links
        side = 0 if d < 0 else 1
        there = jnp.clip(k.z - d, 0, k.layers - 1)
        return k.remote(
            self.held(d, s - 1), self.relayed[d, s], self.z_send.at[side, s],
            self.z_recv.at[side, s], there * k.plane + k.q,
        )

    def spread(self, layer, e):
        k = self.links
        return k.remote(
            self.send.at[layer, e], self.near.at[layer * k.plane + k.q],
            self.p_send.at[layer, e], self.p_recv.at[layer, e], k.z * k.plane + k.qs[e],
        )

    def pack(self, d, s, e):
        k = self.links
        source, layer = self.held(d, s), self.layer(d, s)

        def put(spot, value):
            if e == 0:
                self.near[layer * k.plane + k.q, spot] = value
            else:
                self.send[layer, e, spot] = value

        if self.tail:
            row = lax.broadcasted_iota(jnp.int32, (TAIL, 128), 0)
            tile = jnp.zeros((TAIL, 128), f32)
            every = source[self.last].astype(f32)
        for c in range(self.capacity):
            index = jnp.maximum(self.table.asked(k.qs[e], layer, c), 0)
            for i in range(self.tiles):
                put(c * self.tiles + i, source[index * self.tiles + i])
            if self.tail:
                line = jnp.sum(jnp.where(row == index, every, 0.0), axis=0, keepdims=True)
                tile = jnp.where(row == c, line, tile)
        if self.tail:
            put(self.capacity * self.tiles, tile.astype(bf16))

    def serve(self, d, s):
        for e in reversed(range(self.links.plane)):
            self.pack(d, s, e)
            if e:
                self.spread(self.layer(d, s), e).start()

    def start(self):
        for d in (-1, 1):
            @pl.when(inside(self.links.z - d, self.links.layers))
            def _():
                self.hop(d, 0).start()

    def advance(self, d, s):
        z, layers = self.links.z, self.links.layers

        @pl.when(inside(z + d * (s + 1), layers))
        def _():
            self.hop(d, s).wait_recv()
        if s < layers - 2:
            @pl.when(inside(z + d * (s + 1), layers) & inside(z - d, layers))
            def _():
                self.hop(d, s + 1).start()

        @pl.when(inside(z + d * (s + 1), layers))
        def _():
            self.serve(d, s)

    def finish(self):
        for layer in range(self.links.layers):
            for e in range(1, self.links.plane):
                self.spread(layer, e).wait_recv()

    def drain(self):
        z, layers = self.links.z, self.links.layers
        for d in (-1, 1):
            for s in range(layers - 1):
                @pl.when(inside(z - d, layers) & inside(z + d * s, layers))
                def _():
                    self.hop(d, s).wait_send()
        for layer in range(layers):
            for e in range(1, self.links.plane):
                self.spread(layer, e).wait_send()


class Push:
    def __init__(self, links, tables, pick_ref, capacity, refs):
        self.links, self.slot, self.pick, self.capacity = links, tables.slot, pick_ref, capacity
        self.given, self.out, self.arrive, self.zout, self.zin, *sems = refs
        self.z_send, self.z_recv, self.p_send, self.p_recv = sems
        self.group = self.out.shape[1]
        self.tiles = self.group // capacity

    def spread(self, o, e):
        k = self.links
        here = pl.ds(pl.multiple_of(k.q * self.group, self.group), self.group)
        return k.remote(
            self.out.at[k.zs[o] * k.plane + k.qs[e]], self.arrive.at[k.zs[o], here],
            self.p_send.at[o, e], self.p_recv.at[o, e], k.z * k.plane + k.qs[e],
        )

    def hop(self, o):
        k = self.links
        return k.remote(
            self.zout.at[o - 1], self.zin.at[o - 1], self.z_send.at[o - 1],
            self.z_recv.at[o - 1], k.zs[o] * k.plane + k.q,
        )

    def order(self):
        return list(reversed(range(1, self.links.layers)))

    def serve(self, o):
        k = self.links
        for e in reversed(range(k.plane)):
            device = k.zs[o] * k.plane + k.qs[e]
            for c in range(self.capacity):
                index = self.slot(device * self.capacity + c)
                for i in range(self.tiles):
                    value = self.given[index * self.tiles + i]
                    if e:
                        self.out[device, c * self.tiles + i] = value
                    else:
                        self.arrive[k.zs[o], k.q * self.group + c * self.tiles + i] = value
            if e:
                self.spread(o, e).start()

    def gathered(self, o):
        k = self.links
        for e in range(1, k.plane):
            self.spread(o, e).wait_recv()
        arrived = self.arrive[k.zs[o]]
        arrived = arrived.reshape(-1, arrived.shape[-1])
        return dot_nn(self.pick[k.zs[o]], arrived)

    def advance(self, o):
        self.zout[o - 1] = self.gathered(o).astype(bf16)
        self.hop(o).start()

    def finish(self):
        total = self.gathered(0)
        for o in self.order():
            self.hop(o).wait_recv()
            total = total + self.zin[o - 1].astype(f32)
        return total

    def drain(self):
        for o in range(self.links.layers):
            if o:
                self.hop(o).wait_send()
            for e in range(1, self.links.plane):
                self.spread(o, e).wait_send()


def spread_requests(ref, buffer):
    rows, count = ref.shape
    buffer[...] = jnp.zeros_like(buffer)
    buffer[0:rows, 0:count] = ref[...] + 1
    size = buffer.shape[1]
    total = jnp.zeros((size, size), jnp.int32)
    for k in range(rows):
        line = jnp.broadcast_to(buffer[k : k + 1, :], (size, size))
        total = total + (pltpu.roll(line, k * STRIDE, axis=1) if k else line)
    return total


def index_tables(total, layers, capacity, device_ref, slot_ref, buffer, meta_ref):
    plane = total // layers
    size = meta_ref.shape[1]
    lane = lax.broadcasted_iota(jnp.int32, (size, size), 1)
    row = lax.broadcasted_iota(jnp.int32, (size, size), 0)
    devices = spread_requests(device_ref, buffer)
    wanted = jnp.minimum(spread_requests(slot_ref, buffer), slot_ref.shape[1]).T
    target = lax.axis_index("rows") - devices
    target = jnp.where(target < 0, target + total, target)
    target = jnp.where(devices > 0, target, -1)
    other = target.T
    before = jnp.where((target == other) & (row < lane), 1, 0)
    rank = jnp.minimum(jnp.sum(before, axis=0, keepdims=True), capacity - 1)
    rank = jnp.broadcast_to(rank, (size, size))
    lines = [jnp.maximum(target[:1], 0), rank[:1]]
    rank = rank.T
    shift = plane.bit_length() - 1
    ask = ((other & (plane - 1)) * layers + (other >> shift)) * capacity + rank
    ask = jnp.where(other < 0, -1, ask)
    spot = jnp.where(other < 0, -1, other * capacity + rank)
    groups = -(-total * capacity // size)
    for g in range(groups):
        here = jnp.where(spot == lane + g * size, row, 0)
        lines.append(jnp.max(here, axis=0, keepdims=True))
    for g in range(groups):
        here = jnp.where(ask == lane + g * size, wanted, 0)
        lines.append(jnp.max(here, axis=0, keepdims=True) - 1)
    line_row = lax.broadcasted_iota(jnp.int32, meta_ref.shape, 0)
    tile = jnp.zeros(meta_ref.shape, jnp.int32)
    for i, line in enumerate(lines):
        tile = jnp.where(line_row == i, line, tile)
    meta_ref[...] = tile


class Tables:
    def __init__(self, links, table_ref, capacity):
        self.links, self.ref, self.capacity = links, table_ref, capacity
        self.size = table_ref.shape[2]
        self.groups = -(-links.layers * links.plane * capacity // self.size)

    def target(self, n, k):
        return self.ref[self.links.q, 0, k * STRIDE + n]

    def rank(self, n, k):
        return self.ref[self.links.q, 1, k * STRIDE + n]

    def slot(self, i):
        return self.ref[self.links.q, 2 + i // self.size, lax.rem(i, self.size)]

    def asked(self, other, layer, c):
        i = (self.links.q * self.links.layers + layer) * self.capacity + c
        return self.ref[other, 2 + self.groups + i // self.size, lax.rem(i, self.size)]


def whole_kernel(
    geometry, factor, scale, counts,
    noise_ref, shift_ref, c_source, v_ref, device_ref, slot_ref,
    result_ref, *scratch,
):
    total, layers, capacity = geometry
    count, size, _ = noise_ref.shape
    vec = v_ref.shape[0]
    half = size // 2
    scratch = list(scratch)
    take = lambda k: [scratch.pop(0) for _ in range(k)]
    d_ref, e_ref, u_ref, p_ref, rest_ref, m, pscr, qscr = take(8)
    pad = m.shape[0] // size
    links = Links(total, layers)
    pick_ref, buffer, meta_ref, ask_in, table_ref, c_ref = take(6)
    ask_send, ask_recv, table_sem, c_sem = take(4)
    c_copy = pltpu.make_async_copy(c_source, c_ref, c_sem)
    c_copy.start()
    tables = Tables(links, table_ref, capacity)
    shares = vec // TAIL
    split = range(shares)

    def pulls(tails):
        return [Pull(links, tables, capacity, count, tail, take(counts[0])) for tail in tails]

    def pushes():
        return [Push(links, tables, pick_ref, capacity, take(counts[1])) for _ in split]

    pull_e, pull_left, pull_t = pulls((0, 1)), pulls((0,) * shares), pulls((0,) * shares)
    push_w, push_p = pushes(), pushes()

    barrier = pltpu.get_barrier_semaphore()
    for device in links.partners():
        pl.semaphore_signal(barrier, inc=1, device_id=(device,), device_id_type=MESH)

    row_full = lax.broadcasted_iota(jnp.int32, (size, size), 0)
    col_full = lax.broadcasted_iota(jnp.int32, (size, size), 1)
    on_diag = row_full == col_full
    shifts = shift_ref[...].astype(f32)
    for n in range(count):
        noise = noise_ref[n].astype(f32)
        d = (noise + noise.T) * (0.5 * factor)
        d = d + jnp.where(on_diag, shifts[n : n + 1], 0.0)
        d_ref[n] = d
        m[pl.ds(n * size, size), :] = d
        if n < pad - count:
            m[pl.ds((count + n) * size, size), :] = d

    plane = links.plane
    index_tables(total, layers, capacity, device_ref, slot_ref, buffer, meta_ref)

    def ask(e):
        return links.remote(
            meta_ref, ask_in.at[links.q], ask_send.at[e], ask_recv.at[e],
            links.z * plane + links.qs[e],
        )

    def exchange_asks():
        pl.semaphore_wait(barrier, len(links.partners()))
        ask_in[links.q] = meta_ref[...]
        for e in range(1, plane):
            ask(e).start()

    eliminate(m, pscr, qscr, count, pad, size, exchange_asks)
    for e in range(1, plane):
        ask(e).wait()
    table_copy = pltpu.make_async_copy(ask_in, table_ref, table_sem)
    table_copy.start()
    row = lax.broadcasted_iota(jnp.int32, (half, half), 0)
    col = lax.broadcasted_iota(jnp.int32, (half, half), 1)
    tail_row = lax.broadcasted_iota(jnp.int32, (TAIL, size), 0)
    tile = jnp.zeros((TAIL, size), f32)
    parts = half // TAIL // 2
    for n in range(count):
        h, low = split2(m[pl.ds(n * size, size), :])
        e = tdot(jnp.concatenate([h, h, low], axis=0), jnp.concatenate([h, low, h], axis=0))
        e_ref[n] = e.astype(bf16)
        left = jnp.where(row >= col, e[:half, :half], e[half:, half:])
        packed = joined(left, e[:half, half:]).astype(bf16)
        for i in range(parts):
            for j in range(2):
                first = (j * parts + i) * TAIL
                pull_e[j].own[n * parts + i] = packed[first : first + TAIL]
        diag = jnp.sum(jnp.where(on_diag, e, 0.0), axis=0, keepdims=True)
        tile = jnp.where(tail_row == n, diag, tile)
    pull_e[1].own[count * parts] = tile.astype(bf16)

    for pull in pull_e:
        pull.start()
    table_copy.wait()
    for pull in pull_e:
        pull.serve(0, -1)
    width = size // TAIL
    lane = lax.broadcasted_iota(jnp.int32, (TAIL, size), 1)
    same = lax.broadcasted_iota(jnp.int32, (TAIL, size), 0) == lax.rem(lane, TAIL)
    lane = lane // TAIL
    for layer in range(layers):
        for i in range(plane * capacity // width):
            line = jnp.zeros((TAIL, size), jnp.int32)
            for j in range(width):
                other, c = divmod(i * width + j, capacity)
                line = jnp.where(lane == j, tables.asked(other, layer, c), line)
            for n in range(count):
                chosen = jnp.where(same & (line == n), 1.0, 0.0).astype(bf16)
                pick_ref[layer, n * TAIL : (n + 1) * TAIL, i * size : (i + 1) * size] = chosen
    for s in range(layers - 1):
        for pull in pull_e:
            pull.advance(-1, s)
            pull.advance(1, s)
    for pull in pull_e:
        pull.finish()

    c_copy.wait()

    def schur(n, carry):
        fs, cs = [], []
        for k in range(3):
            t = tables.target(n, k)
            c = tables.rank(n, k)
            packed = jnp.concatenate(
                [pull.near[t, c * parts + i] for pull in pull_e for i in range(parts)], axis=0
            ).astype(f32)
            tile = pull_e[1].near[t, capacity * parts].astype(f32)
            diag = jnp.sum(jnp.where(tail_row == c, tile, 0.0), axis=0, keepdims=True)
            flipped = packed.T
            part = packed[:, :half]
            part_t = flipped[:half, :]
            first = jnp.where(row >= col, part, part_t)
            last = jnp.where(row < col, part, part_t)
            last = jnp.where(row == col, diag[:, half:], last)
            inverse = jnp.concatenate(
                [joined(first, packed[:, half:]), joined(flipped[half:, :], last)], axis=0
            ).astype(bf16)
            coupling = c_ref[n, k]
            fs.append((dot_nn(coupling, inverse) * (scale * scale)).astype(bf16))
            cs.append(coupling)
        reduced = d_ref[n] - dot_nt(joined(*fs), joined(*cs))
        m[pl.ds(pl.multiple_of(n * size, size), size), :] = reduced
        return carry

    lax.fori_loop(0, count, schur, 0, unroll=UNROLL)
    for n in range(count, pad):
        m[pl.ds(n * size, size), :] = d_ref[0]
    eliminate(m, pscr, qscr, count, pad, size)

    def give(push, n, x):
        low = (x * scale).astype(bf16)
        for k in range(3):
            value = dot_nn(low, c_ref[n, k]).astype(bf16)
            for i, part in enumerate(push):
                part.given[k * STRIDE + n] = value[i * TAIL : (i + 1) * TAIL]

    def pulled(pull, n):
        got = [pull.near[tables.target(n, k), tables.rank(n, k)] for k in range(3)]
        return scale * dot_nt(joined(*got), joined(*[c_ref[n, k] for k in range(3)]))

    for n in range(count):
        kh, kl = split2(m[pl.ds(n * size, size), :])
        vh, vl = split2(v_ref[:, n * size : (n + 1) * size])
        u = dot_nn(joined(vh, vh, vl), jnp.concatenate([kh, kl, kh], axis=0))
        u_ref[n] = u
        give(push_w, n, u)
    for push in push_w:
        for o in push.order() + [0]:
            push.serve(o)
    for n in range(count):
        uh, ul = split2(u_ref[n])
        dh, dl = split2(d_ref[n])
        rest_ref[n] = dot_nn(joined(uh, uh, ul), jnp.concatenate([dh, dl, dh], axis=0))
    for push in push_w:
        for o in push.order():
            push.advance(o)

    span = [slice(i * TAIL, (i + 1) * TAIL) for i in split]
    for i in split:
        w = push_w[i].finish().astype(bf16)
        for n in range(count):
            p = dot_nn(w[n * TAIL : (n + 1) * TAIL], e_ref[n])
            p_ref[n, span[i], :] = p
            pull_left[i].own[n] = (u_ref[n, span[i], :] - p).astype(bf16)
            give(push_p[i : i + 1], n, p)
        pull_left[i].start()
        for o in push_p[i].order() + [0]:
            push_p[i].serve(o)
        pull_left[i].serve(0, -1)
    for i in split:
        for s, o in enumerate(push_p[i].order()):
            push_p[i].advance(o)
            pull_left[i].advance(-1, s)
            pull_left[i].advance(1, s)
    for i in split:
        pushed = push_p[i].finish()
        pull_left[i].finish()
        for n in range(count):
            sent = pushed[n * TAIL : (n + 1) * TAIL]
            q = pulled(pull_left[i], n) - sent
            t = p_ref[n, span[i], :] + dot_nn(q.astype(bf16), e_ref[n])
            pull_t[i].own[n] = t.astype(bf16)
            rest_ref[n, span[i], :] = rest_ref[n, span[i], :] - sent
        pull_t[i].start()
        pull_t[i].serve(0, -1)
    for i in split:
        for s in range(layers - 1):
            pull_t[i].advance(-1, s)
            pull_t[i].advance(1, s)
    for i in split:
        pull_t[i].finish()
        for n in range(count):
            part = rest_ref[n, span[i], :] - pulled(pull_t[i], n)
            ph, plow = split2(part)
            kh, kl = split2(m[pl.ds(n * size, size), :])
            result_ref[span[i], n * size : (n + 1) * size] = dot_nt(
                joined(ph, ph, plow), joined(kh, kl, kh)
            )
    for moved in pull_e + push_w + push_p + pull_left + pull_t:
        moved.drain()


def run(geometry, factor, scale, arrays, row_count, block_size, vec_count):
    total, layers, capacity = geometry
    plane = total // layers
    vmem = pl.BlockSpec(memory_space=pltpu.VMEM)
    apart = pl.BlockSpec(memory_space=pl.ANY)
    dma = pltpu.SemaphoreType.DMA
    pad = -(-row_count // 8) * 8
    block_shape = (row_count, block_size, block_size)
    rows_shape = (row_count, vec_count, block_size)
    scratch = [
        pltpu.VMEM(block_shape, f32),
        pltpu.VMEM(block_shape, bf16),
        pltpu.VMEM(rows_shape, f32),
        pltpu.VMEM(rows_shape, f32),
        pltpu.VMEM(rows_shape, f32),
        pltpu.VMEM((pad * block_size, block_size), f32),
        pltpu.VMEM((PANEL * pad, block_size), f32),
        pltpu.VMEM((PANEL * pad, block_size), f32),
    ]
    scratch += [
        pltpu.VMEM((layers, row_count * TAIL, plane * capacity * TAIL), bf16),
        pltpu.VMEM((8, block_size), jnp.int32),
        pltpu.VMEM((8, block_size), jnp.int32),
        pltpu.VMEM((plane, 8, block_size), jnp.int32),
        pltpu.SMEM((plane, 8, block_size), jnp.int32),
        pltpu.VMEM((row_count, 3, block_size, block_size), bf16),
        dma((plane,)),
        dma((plane,)),
        dma,
        dma,
    ]
    shares = vec_count // TAIL
    pull_count = push_count = 0

    def tiles(*shape):
        return pltpu.VMEM(shape + (TAIL, block_size), bf16)

    quarter = block_size // 4 // TAIL
    for parts, tail in ((quarter, 0), (quarter, 1)) + ((1, 0),) * (2 * shares):
        own, group = row_count * parts + tail, capacity * parts + tail
        pulls = [tiles(own), tiles(layers, plane, group), tiles(total, group)]
        pulls += [tiles(own)] * (2 * layers - 2)
        pulls += [dma((2, layers - 1))] * 2 + [dma((layers, plane))] * 2
        pull_count = len(pulls)
        scratch += pulls
    for _ in range(2 * shares):
        pushes = [tiles(3 * STRIDE), tiles(total, capacity), tiles(layers, plane * capacity)]
        pushes += [pltpu.VMEM((layers - 1, row_count * TAIL, block_size), bf16)] * 2
        pushes += [dma((layers - 1,))] * 2 + [dma((layers, plane))] * 2
        push_count = len(pushes)
        scratch += pushes
    return pl.pallas_call(
        functools.partial(whole_kernel, geometry, factor, scale, (pull_count, push_count)),
        out_shape=jax.ShapeDtypeStruct((vec_count, row_count * block_size), f32),
        in_specs=[vmem, vmem, apart, vmem, vmem, vmem],
        out_specs=vmem,
        scratch_shapes=scratch,
        compiler_params=pltpu.CompilerParams(collective_id=0, has_side_effects=True),
    )(*arrays)


def body(diag_noise, couplings, shifts, near_devices, near_slots, vectors):
    dev_count = lax.axis_size("rows")
    row_count, block_size = diag_noise.shape[:2]
    vec_count = vectors.shape[0]
    capacity = 3 * row_count // (dev_count - 1) + 2
    layers = LAYERS
    factor = 0.5 / math.sqrt(block_size)
    scale = 0.4 / math.sqrt(block_size)

    return run(
        (dev_count, layers, capacity), factor, scale,
        (diag_noise, shifts, couplings, vectors, near_devices.T, near_slots.T),
        row_count, block_size, vec_count,
    )


def solution(mesh):
    return jax.shard_map(
        body,
        mesh=mesh,
        in_specs=(
            P("rows", None, None),
            P("rows", None, None, None),
            P("rows", None),
            P("rows", None),
            P("rows", None),
            P(None, "rows"),
        ),
        out_specs=P(None, "rows"),
        check_vma=False,
    )
```
